32 devices in a mesh: grp: 2 (over x), date: 16 (over z, y, core).
Axes of the slice: x: 2, y: 2, z: 4, core: 2. Of those that a mesh axis runs over, the one named last changes fastest.
Arguments:
- radar_stack: bfloat16 [2, 128, 256, 256], P(None, 'date', 'grp'), parts along dimension 2, may hold values from -6 to 6
- filter_taps: float32 [2, 128, 128], P(None, 'date'), may hold values from -0.6 to 0.6
- filter_lengths: int32 [128], P('date'), may hold values from 64 to 128
- resample_kernel: float32 [4], replicated, may hold values from 0.2 to 1
- tile_owner: int32 [512, 1], P(('grp', 'date')), parts along dimension 0, may hold values from 0 to 15; in each aligned block of 16 rows (0 to 15, 16 to 31, ...) at most 2 rows name the same one
- map_slot: int32 [512], P(('grp', 'date')), parts along dimension 0, may hold values from 0 to 7
- correlation: int32 [512], P(('grp', 'date')), parts along dimension 0, may hold values from 1 to 128
- offsets: int32 [512], P(('grp', 'date')), parts along dimension 0, may hold values from 0 to 127
Outputs:
- geocoded: float32 [256, 256, 128], P(('grp', 'date')), parts along dimension 0
The draws below stay inside these ranges and needn't reach their ends.
There are 2 independent parts, one for each index of `grp`. The reference program is written for one: setup_inputs(seed, part) draws one part's arguments, and reference() takes and returns one part's arrays. A program takes and returns all parts, laid end to end along the dimension named above; an argument that names none is the same for every part. Nothing has to cross between parts.
Inputs may be any that keep to these rules, and one draw needn't show every extreme that they name: `tile_owner`: among the 16 tiles of one device, at most 2 name the same owner.
All inputs are finite; a program needn't handle non-finite values. Where the reference program divides by a largest or mean magnitude, that divisor is 1e-20 or more.
Results may differ from the reference program's by a relative error of at most 0.0055.
Values may be sent and summed in bfloat16 or wider, within the bound.
A program may use at most 64 MiB of HBM per device.

```python
import math
import jax
import jax.numpy as jnp
import numpy as np
from jax import lax

DATES = 128
TAPS = 128
RG = 256
PATCH_AZ = 8
PATCH_RG = 16
SWEEPS = 3
TILE = 128
KW = 4
CAP = 2
MAP_DEV = 8
AZ = 128
TILES_DEV = 16
TILES = 256
MAP_TILES = 128
N_DATE = 16


def place_ends(array, key, least, largest):
    extent = array.shape
    index_at = [jax.random.randint(jax.random.fold_in(key, axis), (), 0, extent[axis]) for axis in range(len(extent))]
    array = array.at[tuple(index_at)].set(least)
    longest = extent.index(max(extent))
    index_at[longest] = (index_at[longest] + 1) % extent[longest]
    return array.at[tuple(index_at)].set(largest)


def level_of(stream_key, extent, shards, smallest, largest):
    loudness, own = 1.0, jax.random.fold_in(stream_key, 6)
    for dim, shards_of in shards:
        draws = jnp.exp(jax.random.uniform(jax.random.fold_in(own, dim), (shards_of,), jnp.float32, smallest / len(shards), largest / len(shards)))
        loudness = loudness * jnp.repeat(draws, extent[dim] // shards_of).reshape([-1 if axis == dim else 1 for axis in range(len(extent))])
    return loudness


def assign_block(own_key, own, number, rows, amount, top, most, slope):
    ranking = jax.random.permutation(own_key, amount)
    packed, common = shares(amount, rows * top, most, slope, True), shares(amount, rows * top, most, slope, False)
    places = jnp.arange(amount)

    def named(sizes, turn):
        used = int((sizes > 0).sum())
        fixed = max(1, used // 4)
        passed = fixed + (places - fixed + turn * (used - fixed)) % max(1, amount - fixed)
        return jnp.zeros((amount,), jnp.int32).at[ranking[jnp.where(places < fixed, places, passed)]].set(jnp.asarray(sizes, jnp.int32))

    sizes = jnp.where(number % 4 == 0, named(packed, number // 4), named(common, number - number // 4 - 1))
    mixed = jax.random.permutation(jax.random.fold_in(own, 3), amount)
    source_of, taker = mixed[0:amount // 2 * 2:2], mixed[1:amount // 2 * 2:2]
    room = jnp.minimum(sizes[source_of] - 1, most - sizes[taker]) // 2
    room = jnp.where((source_of == ranking[0]) | (taker == ranking[0]) | (sizes[taker] == 0), 0, jnp.maximum(room, 0))
    passed = jax.random.randint(jax.random.fold_in(own, 4), (amount // 2,), 0, 1 << 20) % (room + 1)
    sizes = sizes.at[source_of].add(-passed).at[taker].add(passed)
    items = jnp.searchsorted(jnp.cumsum(sizes), jnp.arange(rows * top), side="right").astype(jnp.int32)
    listing = items.reshape(top, rows).T
    listing = listing[jax.random.permutation(jax.random.fold_in(own, 1), rows)]
    turn = jax.random.randint(jax.random.fold_in(own, 2), (rows, 1), 0, top)
    return jnp.take_along_axis(listing, (jnp.arange(top)[None, :] + turn) % top, axis=1)


def shares(number_of, total, reach, lean, full):
    loads = [(1 << 20) // math.isqrt(rank ** lean) + 1 for rank in range(1, number_of + 1)]
    largest = reach if full else min(reach, max(-(-total // number_of), total * loads[0] // sum(loads)))
    least = 1 if total - largest >= number_of - 1 else 0
    given, rest = [largest] + [least] * (number_of - 1), total - largest - least * (number_of - 1)
    while rest > 0:
        candidates = [i for i in range(1, number_of) if given[i] < largest] or [i for i in range(1, number_of) if given[i] < reach]
        mass, remaining = sum([loads[i] for i in candidates]), rest
        for i in candidates:
            more = min(reach - given[i], max(1, remaining * loads[i] // mass), rest)
            given[i] = given[i] + more
            rest = rest - more
    return np.array(given)


def gaussian(key, shape, scale, bound, cuts=(), kind=jnp.bfloat16):
    drawn = scale * jax.random.normal(key, shape, jnp.float32)
    if cuts:
        drawn = drawn * level_of(key, shape, cuts, -0.22, 0.18)
    return jnp.clip(drawn, -bound, bound).astype(kind)


def setup_inputs(seed: int = 0, part: int = 0) -> dict:
    streams_of = jax.random.split(jax.random.key(seed), 9)
    part_keys = jax.random.split(jax.random.fold_in(streams_of[8], part), 9)
    radar_stack = gaussian(part_keys[0], (2, DATES, AZ, RG), 1.0, 6.0, ((1, 16),))
    filter_taps = gaussian(streams_of[1], (2, DATES, TAPS), 0.1, 0.6, ((1, 16),), jnp.float32)
    filter_lengths = place_ends(jax.random.randint(streams_of[2], (DATES,), TAPS // 2, TAPS + 1), jax.random.fold_in(streams_of[2], 1), TAPS // 2, TAPS).astype(jnp.int32)
    resample_kernel = jnp.clip(jax.random.uniform(streams_of[3], (KW,), jnp.float32, 0.2, 1.0), 0.2, 1.0)
    tile_owner_keys = jax.random.split(jax.random.fold_in(part_keys[4], 1), TILES // TILES_DEV)
    tile_owner_turns = jax.random.permutation(jax.random.fold_in(part_keys[4], 3), TILES // TILES_DEV)
    tile_owner = jax.vmap(lambda own, number: assign_block(jax.random.fold_in(part_keys[4], 2), own, number, TILES_DEV, N_DATE, 1, CAP, 2))(tile_owner_keys, tile_owner_turns).reshape((TILES, 1))
    map_slot = place_ends(jax.random.randint(part_keys[5], (TILES,), 0, MAP_DEV), jax.random.fold_in(part_keys[5], 1), 0, MAP_DEV - 1).astype(jnp.int32)
    correlation = place_ends(jax.random.randint(part_keys[6], (TILES,), 1, TILE + 1), jax.random.fold_in(part_keys[6], 1), 1, TILE).astype(jnp.int32)
    offsets = place_ends(jax.random.randint(part_keys[7], (TILES,), 0, TILE), jax.random.fold_in(part_keys[7], 1), 0, TILE - 1).astype(jnp.int32)
    return {"radar_stack": radar_stack, "filter_taps": filter_taps, "filter_lengths": filter_lengths, "resample_kernel": resample_kernel, "tile_owner": tile_owner, "map_slot": map_slot, "correlation": correlation, "offsets": offsets}


diag_load = 0.5
small_eps = 1e-05
highest = lax.Precision.HIGHEST

def toeplitz_matrix(taps_one, length_one, rows_count):
    positions = jnp.arange(TAPS, dtype=jnp.int32)
    masked = jnp.where(positions < length_one, taps_one, jnp.zeros_like(taps_one))
    period = 2 * rows_count - 1
    padded = jnp.pad(masked, (0, period - TAPS))
    wrapped = jnp.roll(padded, -(TAPS // 2))
    flat_rows = jnp.tile(wrapped, rows_count)[:rows_count * (period - 1)]
    return flat_rows.reshape(rows_count, period - 1)[:, :rows_count]

def block_operator(taps_date, length_one, rows_count):
    real_mat = toeplitz_matrix(taps_date[0], length_one, rows_count)
    imag_mat = toeplitz_matrix(taps_date[1], length_one, rows_count)
    upper = jnp.concatenate([real_mat, -imag_mat], axis=1)
    lower = jnp.concatenate([imag_mat, real_mat], axis=1)
    return jnp.concatenate([upper, lower], axis=0).astype(jnp.bfloat16)

def complex_product(left_re, left_im, right_re, right_im):

    def mult(first, second):
        return jnp.einsum('pij,pjk->pik', first, second, precision=highest)
    return (mult(left_re, right_re) - mult(left_im, right_im), mult(left_re, right_im) + mult(left_im, right_re))

def whiten_patches(patches):
    values = patches.astype(jnp.float32)
    z_re = values[:, 0]
    z_im = values[:, 1]
    date_count = patches.shape[2]
    look_count = patches.shape[3]
    gram_re = (jnp.einsum('pil,pjl->pij', z_re, z_re, precision=highest) + jnp.einsum('pil,pjl->pij', z_im, z_im, precision=highest)) / look_count
    gram_im = (jnp.einsum('pil,pjl->pij', z_im, z_re, precision=highest) - jnp.einsum('pil,pjl->pij', z_re, z_im, precision=highest)) / look_count
    diagonal = jnp.diagonal(gram_re, axis1=1, axis2=2)
    scaled = lax.rsqrt(diagonal + small_eps)
    outer_scale = scaled[:, :, None] * scaled[:, None, :]
    identity = jnp.eye(date_count, dtype=jnp.float32)
    coher_re = gram_re * outer_scale + diag_load * identity[None]
    coher_im = gram_im * outer_scale
    row_bound = lax.optimization_barrier(jnp.max(lax.optimization_barrier(jnp.sum(jnp.abs(coher_re) + jnp.abs(coher_im), axis=2)), axis=1))
    inverse_re = identity[None] / row_bound[:, None, None]
    inverse_im = jnp.zeros_like(coher_im)
    for _ in range(SWEEPS):
        prod_re, prod_im = complex_product(coher_re, coher_im, inverse_re, inverse_im)
        corr_re, corr_im = complex_product(inverse_re, inverse_im, prod_re, prod_im)
        inverse_re = 2.0 * inverse_re - corr_re
        inverse_im = 2.0 * inverse_im - corr_im
    white_re, white_im = complex_product(inverse_re, inverse_im, z_re, z_im)
    return jnp.stack([white_re, white_im], axis=1).astype(jnp.bfloat16)

def to_patches(field):
    date_count = field.shape[1]
    rows_count = field.shape[2]
    ranges_count = field.shape[3]
    blocks = field.reshape(2, date_count, rows_count // PATCH_AZ, PATCH_AZ, ranges_count // PATCH_RG, PATCH_RG)
    return blocks.transpose(2, 4, 0, 1, 3, 5).reshape(-1, 2, date_count, PATCH_AZ * PATCH_RG)

def from_patches(patches, rows_count, ranges_count):
    date_count = patches.shape[2]
    blocks = patches.reshape(rows_count // PATCH_AZ, ranges_count // PATCH_RG, 2, date_count, PATCH_AZ, PATCH_RG)
    return blocks.transpose(2, 3, 0, 4, 1, 5).reshape(2, date_count, rows_count, ranges_count)

def to_tiles(field):
    date_count = field.shape[1]
    rows_count = field.shape[2]
    ranges_count = field.shape[3]
    blocks = field.reshape(2, date_count, rows_count, ranges_count // TILE, TILE)
    return blocks.transpose(2, 3, 0, 1, 4).reshape(-1, 2 * date_count, TILE)

def resample_tiles(tiles, shifts, resample_kernel):
    rounded = lax.optimization_barrier(resample_kernel.astype(jnp.bfloat16)).astype(jnp.float32)
    column = jnp.arange(TILE, dtype=jnp.int32)
    first_cell = column[None, :] + shifts.astype(jnp.int32)[:, None]
    matrix = jnp.zeros((shifts.shape[0], TILE, TILE), jnp.float32)
    for tap_index in range(KW):
        source = (first_cell + tap_index) % TILE
        matrix = matrix + rounded[tap_index] * (column[None, None, :] == source[:, :, None]).astype(jnp.float32)
    return jnp.einsum('sji,sci->scj', matrix, tiles.astype(jnp.float32), precision=highest)

def reference(radar_stack, filter_taps, filter_lengths, resample_kernel, tile_owner, map_slot, correlation, offsets):
    rows_count = radar_stack.shape[2]
    ranges_count = radar_stack.shape[3]

    def filter_one(operands):
        taps_date, length_one, columns = operands
        operator = block_operator(taps_date, length_one, rows_count).astype(jnp.float32)
        flat_cols = columns.reshape(2 * rows_count, ranges_count).astype(jnp.float32)
        product = jnp.dot(operator, flat_cols, precision=highest)
        return product.reshape(2, rows_count, ranges_count).astype(jnp.bfloat16)
    filtered = lax.map(filter_one, (filter_taps.transpose(1, 0, 2), filter_lengths, radar_stack.transpose(1, 0, 2, 3)))
    filtered = filtered.transpose(1, 0, 2, 3)
    patches = to_patches(filtered)
    grouped = patches.reshape((N_DATE, -1) + patches.shape[1:])
    whitened = lax.map(whiten_patches, grouped).reshape(patches.shape)
    field = from_patches(whitened, rows_count, ranges_count)
    tiles = to_tiles(field)
    tile_count = tiles.shape[0]
    resampled = resample_tiles(tiles, offsets, resample_kernel).reshape(tile_count, -1)
    targets = tile_owner[:, 0] * MAP_DEV + map_slot
    map_iota = jnp.arange(MAP_TILES, dtype=jnp.int32)
    spread = jnp.where(targets[None, :] == map_iota[:, None], correlation.astype(jnp.float32)[None, :], jnp.zeros((), jnp.float32))
    total = jnp.dot(spread, resampled, precision=highest)
    denominator = jnp.maximum(lax.optimization_barrier(jnp.sum(spread, axis=1)), 1.0)
    return (total / denominator[:, None]).reshape(MAP_TILES, 2 * DATES, TILE)
```

```python
from functools import partial

import jax
import jax.numpy as jnp
from jax import lax
from jax.experimental import pallas as pl
from jax.experimental.pallas import tpu as pltpu
from jax.sharding import PartitionSpec as P

PATCH_AZ = 8
PATCH_RG = 16
TILE = 128
KW = 4
CAP = 2
MAP_DEV = 8
LANES = 128

diag_load = 0.5
small_eps = 1e-05
MESH = pl.DeviceIdType.MESH
VMEM = pl.BlockSpec(memory_space=pltpu.VMEM)
SMEM = pl.BlockSpec(memory_space=pltpu.SMEM)
BIG = 60 * 1024 * 1024


def block_transpose(parts, group):
    count = len(parts)
    lane = lax.broadcasted_iota(jnp.int32, parts[0].shape, 1) // group
    bit = 1
    while bit < count:
        low = (lane // bit) % 2 == 0
        new = list(parts)
        for a in range(count):
            if a & bit == 0:
                x, y = parts[a], parts[a | bit]
                new[a] = jnp.where(low, x, pltpu.roll(y, bit * group, 1))
                new[a | bit] = jnp.where(low, pltpu.roll(x, LANES - bit * group, 1), y)
        parts = new
        bit *= 2
    return parts


def filter_kernel(n, len_ref, radar_ref, taps_ref, out_ref, rows_ref):
    dates, rows = radar_ref.shape[1], radar_ref.shape[2]
    taps = taps_ref.shape[2]
    halves = out_ref.shape[1]
    position = lax.broadcasted_iota(jnp.int32, (1, taps), 1)
    a_iota = lax.broadcasted_iota(jnp.int32, (rows, rows), 0)
    b_iota = lax.broadcasted_iota(jnp.int32, (rows, rows), 1)
    at = b_iota - a_iota + taps // 2
    inside = jnp.logical_and(at >= 0, at < taps)
    for d in range(dates):

        def toeplitz(which):
            h = jnp.where(position < len_ref[d], taps_ref[which, pl.ds(d, 1), :], 0.0)
            wide = jnp.broadcast_to(h, (rows, taps))
            rolled = pltpu.roll(wide, taps // 2, 1, stride=1, stride_axis=0)
            full = jnp.concatenate([rolled] * (rows // taps), axis=1)
            return jnp.where(inside, full, 0.0)

        t_re, t_im = toeplitz(0), toeplitz(1)
        operator = jnp.concatenate(
            [jnp.concatenate([t_re, -t_im], axis=1), jnp.concatenate([t_im, t_re], axis=1)], axis=0
        ).astype(jnp.bfloat16)
        columns = jnp.concatenate([radar_ref[0, d], radar_ref[1, d]], axis=0)
        product = jnp.dot(operator, columns, preferred_element_type=jnp.float32)
        for c in range(halves):
            for p in range(n):
                for part in range(2):
                    top = part * rows + p * PATCH_AZ
                    rows_ref[c, p, pl.ds(part * PATCH_AZ * dates + d, PATCH_AZ, stride=dates), :] = (
                        product[top : top + PATCH_AZ, c * LANES : (c + 1) * LANES]
                    )
    for c in range(halves):
        for p in range(n):
            out_ref[p, c] = rows_ref[c, p].astype(jnp.bfloat16)


def exchange_kernel(n, count, *refs):
    ins, outs = refs[:count], refs[count : 2 * count]
    send_sem, recv_sem, own_sem = refs[2 * count :]
    me = lax.axis_index("date")
    barrier = pltpu.get_barrier_semaphore()
    for k in range(1, n):
        peer = lax.rem(me + k, n)
        pl.semaphore_signal(barrier, inc=1, device_id={"date": peer}, device_id_type=MESH)
    own = [
        pltpu.make_async_copy(x.at[me], y.at[me], own_sem.at[i])
        for i, (x, y) in enumerate(zip(ins, outs))
    ]
    for copy in own:
        copy.start()
    pl.semaphore_wait(barrier, n - 1)

    def outgoing(i, peer):
        return pltpu.make_async_remote_copy(
            src_ref=ins[i].at[peer],
            dst_ref=outs[i].at[me],
            send_sem=send_sem.at[i, peer],
            recv_sem=recv_sem.at[i, me],
            device_id={"date": peer},
            device_id_type=MESH,
        )

    def incoming(i, peer):
        return pltpu.make_async_remote_copy(
            src_ref=ins[i].at[peer],
            dst_ref=outs[i].at[peer],
            send_sem=send_sem.at[i, peer],
            recv_sem=recv_sem.at[i, peer],
            device_id={"date": peer},
            device_id_type=MESH,
        )

    for k in range(1, n):
        for i in range(count):
            outgoing(i, lax.rem(me + k, n)).start()
    for k in range(1, n):
        for i in range(count):
            incoming(i, lax.rem(me + n - k, n)).wait_recv()
    for k in range(1, n):
        for i in range(count):
            outgoing(i, lax.rem(me + k, n)).wait_send()
    for copy in own:
        copy.wait()


def exchange(n, collective, *arrays):
    count = len(arrays)
    return pl.pallas_call(
        partial(exchange_kernel, n, count),
        out_shape=[jax.ShapeDtypeStruct(x.shape, x.dtype) for x in arrays],
        in_specs=[VMEM] * count,
        out_specs=[VMEM] * count,
        scratch_shapes=[
            pltpu.SemaphoreType.DMA((count, n)),
            pltpu.SemaphoreType.DMA((count, n)),
            pltpu.SemaphoreType.DMA((count,)),
        ],
        compiler_params=pltpu.CompilerParams(collective_id=collective, has_side_effects=True, vmem_limit_bytes=BIG),
        name="exchange%d" % collective,
    )(*arrays)


def whiten_window(z):
    dates, looks = z.shape[0] // 2, z.shape[1]
    gram = lax.dot_general(z, z, (((1,), (1,)), ((), ())), preferred_element_type=jnp.float32)
    gram_re = (gram[:dates, :dates] + gram[dates:, dates:]) * (1.0 / looks)
    gram_im = (gram[dates:, :dates] - gram[:dates, dates:]) * (1.0 / looks)
    eye = lax.broadcasted_iota(jnp.int32, (dates, dates), 0) == lax.broadcasted_iota(
        jnp.int32, (dates, dates), 1
    )
    diagonal = jnp.where(eye, gram_re, 0.0)
    scale_col = lax.rsqrt(jnp.sum(diagonal, axis=1, keepdims=True) + small_eps)
    scale_row = lax.rsqrt(jnp.sum(diagonal, axis=0, keepdims=True) + small_eps)
    outer = scale_col * scale_row
    coher_re = gram_re * outer + jnp.where(eye, diag_load, 0.0)
    coher_im = gram_im * outer
    sums = jnp.sum(jnp.abs(coher_re) + jnp.abs(coher_im), axis=1, keepdims=True)
    over = 1.0 / jnp.max(sums, axis=0, keepdims=True)

    def embed(re, im):
        re, im = re.astype(jnp.bfloat16), im.astype(jnp.bfloat16)
        top = jnp.concatenate([re, -im], axis=1)
        return top, jnp.concatenate([top, jnp.concatenate([im, re], axis=1)], axis=0)

    part_re, part_im = coher_re * over, coher_im * over
    stages = []
    for stage in range(3):
        top, whole = embed(part_re, part_im)
        stages.append(whole)
        if stage < 2:
            square = jnp.dot(top, whole, preferred_element_type=jnp.float32)
            part_re = 2.0 * part_re - square[:, :dates]
            part_im = 2.0 * part_im + square[:, dates:]
    w = z.astype(jnp.float32)
    for whole in reversed(stages):
        w = 2.0 * w - jnp.dot(whole, w.astype(jnp.bfloat16), preferred_element_type=jnp.float32)
    return w * over


def whiten_kernel(n, table_ref, x_ref, out_ref, z_ref, tiles_ref):
    halves, rows = x_ref.shape[1], x_ref.shape[2]
    dates_here = rows // (2 * PATCH_AZ)
    total = n * dates_here
    per_half = LANES // PATCH_RG
    for s in range(n):
        for c in range(halves):
            x = x_ref[s, c].astype(jnp.float32)
            lines = []
            for a in range(PATCH_AZ):
                re = x[a * dates_here : (a + 1) * dates_here]
                start = PATCH_AZ * dates_here + a * dates_here
                lines.append(jnp.concatenate([re, x[start : start + dates_here]], axis=0))
            for j, window in enumerate(block_transpose(lines, PATCH_RG)):
                z_ref[c * per_half + j, pl.ds(s * dates_here, dates_here), :] = window[:dates_here]
                z_ref[c * per_half + j, pl.ds(total + s * dates_here, dates_here), :] = window[dates_here:]
    windows = halves * per_half
    together = 2

    def step(i, carry):
        for q in range(together):
            w = i * together + q
            z_ref[w] = whiten_window(z_ref[w].astype(jnp.bfloat16))
        return carry

    lax.fori_loop(0, windows // together, step, 0)
    chunk = 16

    def back(r, carry):
        at = pl.ds(pl.multiple_of(r * chunk, chunk), chunk)
        for c in range(halves):
            lines = block_transpose([z_ref[c * per_half + j, at, :] for j in range(per_half)], PATCH_RG)
            for a in range(PATCH_AZ):
                tiles_ref[a * halves + c, at, :] = lines[a].astype(jnp.bfloat16)
        return carry

    lax.fori_loop(0, 2 * total // chunk, back, 0)

    def pack(o, carry):
        for i in range(CAP):
            out_ref[o, i] = tiles_ref[table_ref[o * CAP + i]]
        return carry

    lax.fori_loop(0, n, pack, 0)


def resample_kernel_body(slots, slot_ref, shift_ref, corr_ref, kern_ref, x_ref, out_ref, den_ref):
    row = lax.broadcasted_iota(jnp.int32, (TILE, TILE), 0)
    column = lax.broadcasted_iota(jnp.int32, (TILE, TILE), 1)
    apart = row - column + TILE
    for m in range(MAP_DEV):
        out_ref[m] = jnp.zeros(out_ref.shape[1:], jnp.float32)
        den_ref[m] = 0.0
    taps = [kern_ref[k] for k in range(KW)]

    def one(q):
        step = (apart - shift_ref[q]) & (TILE - 1)
        matrix = jnp.zeros((TILE, TILE), jnp.float32)
        for k in range(KW):
            matrix = jnp.where(step == k, taps[k], matrix)
        moved = jnp.dot(
            x_ref[q // CAP, q % CAP], matrix.astype(jnp.bfloat16), preferred_element_type=jnp.float32
        )
        weight = corr_ref[q].astype(jnp.float32)
        m = slot_ref[q]
        out_ref[m] += weight * moved
        den_ref[m] += weight

    def step(i, carry):
        for q in range(CAP):
            one(i * CAP + q)
        return carry

    lax.fori_loop(0, slots // CAP, step, 0)
    for m in range(MAP_DEV):
        out_ref[m] = out_ref[m] / jnp.maximum(den_ref[m], 1.0)


def shards(n, radar_stack, filter_taps, filter_lengths, resample_kernel, tile_owner, map_slot, correlation, offsets):
    dates_here, rows, ranges = radar_stack.shape[1:]
    dates = n * dates_here
    halves = ranges // TILE
    tile_count = tile_owner.shape[0]
    slots = n * CAP
    params = pltpu.CompilerParams(vmem_limit_bytes=BIG)

    owners = tile_owner[:, 0]
    tile_iota = jnp.arange(tile_count, dtype=jnp.int32)
    same = owners[:, None] == owners[None, :]
    rank = jnp.sum(jnp.logical_and(same, tile_iota[None, :] < tile_iota[:, None]), axis=1)
    slot_index = owners * CAP + rank
    placing = (jnp.arange(slots, dtype=jnp.int32)[:, None] == slot_index[None, :]).astype(jnp.int32)
    facts = jnp.stack([tile_iota, map_slot, offsets, correlation], axis=0)
    placed = jnp.sum(placing[None, :, :] * facts[:, None, :], axis=2)
    table = placed[0]
    details = jnp.pad(placed[1:].reshape(3, n, CAP).transpose(1, 0, 2), ((0, 0), (0, 5), (0, LANES - CAP)))

    cells = pl.pallas_call(
        partial(filter_kernel, n),
        out_shape=jax.ShapeDtypeStruct((n, halves, 2 * PATCH_AZ * dates_here, LANES), jnp.bfloat16),
        in_specs=[SMEM, VMEM, VMEM],
        out_specs=VMEM,
        scratch_shapes=[pltpu.VMEM((halves, n, 2 * PATCH_AZ * dates_here, LANES), jnp.float32)],
        compiler_params=params,
        name="filter",
    )(filter_lengths, radar_stack, filter_taps)
    got_cells, got_details = exchange(n, 0, cells, details)
    packed = pl.pallas_call(
        partial(whiten_kernel, n),
        out_shape=jax.ShapeDtypeStruct((n, CAP, 2 * dates, TILE), jnp.bfloat16),
        in_specs=[SMEM, VMEM],
        out_specs=VMEM,
        scratch_shapes=[
            pltpu.VMEM((ranges // PATCH_RG, 2 * dates, LANES), jnp.float32),
            pltpu.VMEM((tile_count, 2 * dates, TILE), jnp.bfloat16),
        ],
        compiler_params=params,
        name="whiten",
    )(table, got_cells)
    (got_tiles,) = exchange(n, 1, packed)
    arrived = got_details[:, :3, :CAP].transpose(1, 0, 2).reshape(3, slots)
    return pl.pallas_call(
        partial(resample_kernel_body, slots),
        out_shape=jax.ShapeDtypeStruct((MAP_DEV, 2 * dates, TILE), jnp.float32),
        in_specs=[SMEM, SMEM, SMEM, SMEM, VMEM],
        out_specs=VMEM,
        scratch_shapes=[pltpu.SMEM((MAP_DEV,), jnp.float32)],
        compiler_params=params,
        name="resample",
    )(arrived[0], arrived[1], arrived[2], resample_kernel, got_tiles)


def solution(mesh):
    in_specs = (
        P(None, "date", "grp", None),
        P(None, "date", None),
        P("date"),
        P(),
        P(("grp", "date"), None),
        P(("grp", "date")),
        P(("grp", "date")),
        P(("grp", "date")),
    )
    out_specs = P(("grp", "date"), None, None)
    return jax.shard_map(
        partial(shards, mesh.shape["date"]), mesh=mesh, in_specs=in_specs, out_specs=out_specs, check_vma=False
    )
```

```python
from functools import partial

import jax
import jax.numpy as jnp
from jax import lax
from jax.experimental import pallas as pl
from jax.experimental.pallas import tpu as pltpu
from jax.sharding import PartitionSpec as P

PATCH_AZ = 8
PATCH_RG = 16
TILE = 128
KW = 4
CAP = 2
MAP_DEV = 8
LANES = 128
PHASES = 2
TOGETHER = 2

diag_load = 0.5
small_eps = 1e-05
MESH = pl.DeviceIdType.MESH
VMEM = pl.BlockSpec(memory_space=pltpu.VMEM)
SMEM = pl.BlockSpec(memory_space=pltpu.SMEM)
BIG = 60 * 1024 * 1024


def block_transpose(parts, group):
    count = len(parts)
    lane = lax.broadcasted_iota(jnp.int32, parts[0].shape, 1) // group
    bit = 1
    while bit < count:
        low = (lane // bit) % 2 == 0
        new = list(parts)
        for a in range(count):
            if a & bit == 0:
                x, y = parts[a], parts[a | bit]
                new[a] = jnp.where(low, x, pltpu.roll(y, bit * group, 1))
                new[a | bit] = jnp.where(low, pltpu.roll(x, LANES - bit * group, 1), y)
        parts = new
        bit *= 2
    return parts


def filter_kernel(n, len_ref, owner_ref, radar_ref, taps_ref, *refs):
    fact_refs, (out_ref, facts_ref, table_ref, rows_ref, seen_ref) = refs[:4], refs[4:]
    dates, rows = radar_ref.shape[1], radar_ref.shape[2]
    taps = taps_ref.shape[2]
    tile_count = owner_ref.shape[0]
    half = LANES // PHASES

    facts_ref[...] = jnp.full(facts_ref.shape, -1, jnp.int32)
    for i, fact in enumerate(fact_refs):
        facts_ref[pl.ds(i, 1), pl.ds(0, tile_count)] = fact[...]
    for o in range(n):
        seen_ref[o] = 0
        for i in range(CAP):
            table_ref[o * CAP + i] = 0
    for t in range(tile_count):
        owner = owner_ref[t]
        rank = seen_ref[owner]
        table_ref[owner * CAP + rank] = t
        seen_ref[owner] = rank + 1

    position = lax.broadcasted_iota(jnp.int32, (1, taps), 1)
    a_iota = lax.broadcasted_iota(jnp.int32, (rows, rows), 0)
    b_iota = lax.broadcasted_iota(jnp.int32, (rows, rows), 1)
    at = b_iota - a_iota + taps // 2
    inside = jnp.logical_and(at >= 0, at < taps)
    low = lax.broadcasted_iota(jnp.int32, (2 * rows, LANES), 1) < half
    for d in range(dates):

        def toeplitz(which):
            h = jnp.where(position < len_ref[d], taps_ref[which, pl.ds(d, 1), :], 0.0)
            wide = jnp.broadcast_to(h, (rows, taps))
            rolled = pltpu.roll(wide, taps // 2, 1, stride=1, stride_axis=0)
            full = jnp.concatenate([rolled] * (rows // taps), axis=1)
            return jnp.where(inside, full, 0.0)

        t_re, t_im = toeplitz(0), toeplitz(1)
        operator = jnp.concatenate(
            [jnp.concatenate([t_re, -t_im], axis=1), jnp.concatenate([t_im, t_re], axis=1)], axis=0
        ).astype(jnp.bfloat16)
        columns = jnp.concatenate([radar_ref[0, d], radar_ref[1, d]], axis=0)
        product = jnp.dot(operator, columns, preferred_element_type=jnp.float32)
        left, right = product[:, :LANES], product[:, LANES:]
        phases = (
            jnp.where(low, left, pltpu.roll(right, half, 1)),
            jnp.where(low, pltpu.roll(left, half, 1), right),
        )
        for h, phase in enumerate(phases):
            for p in range(n):
                for part in range(2):
                    top = part * rows + p * PATCH_AZ
                    rows_ref[h, p, pl.ds(part * PATCH_AZ * dates + d, PATCH_AZ, stride=dates), :] = phase[
                        top : top + PATCH_AZ
                    ]
    for h in range(PHASES):
        for p in range(n):
            out_ref[h, p] = rows_ref[h, p].astype(jnp.bfloat16)


def whiten_window(z):
    dates, looks = z.shape[0] // 2, z.shape[1]
    gram = lax.dot_general(z, z, (((1,), (1,)), ((), ())), preferred_element_type=jnp.float32)
    gram_re = (gram[:dates, :dates] + gram[dates:, dates:]) * (1.0 / looks)
    gram_im = (gram[dates:, :dates] - gram[:dates, dates:]) * (1.0 / looks)
    eye = lax.broadcasted_iota(jnp.int32, (dates, dates), 0) == lax.broadcasted_iota(
        jnp.int32, (dates, dates), 1
    )
    diagonal = jnp.where(eye, gram_re, 0.0)
    scale_col = lax.rsqrt(jnp.sum(diagonal, axis=1, keepdims=True) + small_eps)
    scale_row = lax.rsqrt(jnp.sum(diagonal, axis=0, keepdims=True) + small_eps)
    outer = scale_col * scale_row
    coher_re = gram_re * outer + jnp.where(eye, diag_load, 0.0)
    coher_im = gram_im * outer
    sums = jnp.sum(jnp.abs(coher_re) + jnp.abs(coher_im), axis=1, keepdims=True)
    over = 1.0 / jnp.max(sums, axis=0, keepdims=True)

    def embed(re, im):
        re, im = re.astype(jnp.bfloat16), im.astype(jnp.bfloat16)
        top = jnp.concatenate([re, -im], axis=1)
        return top, jnp.concatenate([top, jnp.concatenate([im, re], axis=1)], axis=0)

    part_re, part_im = coher_re * over, coher_im * over
    stages = []
    for stage in range(3):
        top, whole = embed(part_re, part_im)
        stages.append(whole)
        if stage < 2:
            square = jnp.dot(top, whole, preferred_element_type=jnp.float32)
            part_re = 2.0 * part_re - square[:, :dates]
            part_im = 2.0 * part_im + square[:, dates:]
    w = z.astype(jnp.float32)
    for whole in reversed(stages):
        w = 2.0 * w - jnp.dot(whole, w.astype(jnp.bfloat16), preferred_element_type=jnp.float32)
    return w * over


def flow_kernel(n, table_ref, kern_ref, cells_ref, facts_ref, *refs):
    total_ref, den_ref, got_cells, got_facts, z_ref, tiles_ref, out_msg, got_msg = refs[:8]
    own_sem, fact_send, fact_recv, cell_send, cell_recv, msg_send, msg_recv = refs[8:]
    me = lax.axis_index("date")
    rows = cells_ref.shape[2]
    dates_here = rows // (2 * PATCH_AZ)
    total = n * dates_here
    half = LANES // PHASES
    windows = LANES // PATCH_RG

    barrier = pltpu.get_barrier_semaphore()
    for k in range(1, n):
        pl.semaphore_signal(barrier, inc=1, device_id={"date": lax.rem(me + k, n)}, device_id_type=MESH)
    own = [pltpu.make_async_copy(cells_ref.at[h, me], got_cells.at[h, me], own_sem.at[h]) for h in range(PHASES)]
    own.append(pltpu.make_async_copy(facts_ref, got_facts.at[me], own_sem.at[PHASES]))
    for copy in own:
        copy.start()
    pl.semaphore_wait(barrier, n - 1)

    def remote(src, dst, send, recv, peer):
        return pltpu.make_async_remote_copy(
            src_ref=src, dst_ref=dst, send_sem=send, recv_sem=recv, device_id={"date": peer}, device_id_type=MESH
        )

    def fact_copy(peer, origin):
        return remote(facts_ref, got_facts.at[origin], fact_send.at[peer], fact_recv.at[origin], peer)

    def cell_copy(h, peer, origin):
        return remote(
            cells_ref.at[h, peer], got_cells.at[h, origin], cell_send.at[h, peer], cell_recv.at[h, origin], peer
        )

    def msg_copy(h, peer, origin):
        return remote(
            out_msg.at[h, peer], got_msg.at[h, origin], msg_send.at[h, peer], msg_recv.at[h, origin], peer
        )

    def after(k):
        return lax.rem(me + k, n)

    def before(k):
        return lax.rem(me + n - k, n)

    for h in range(PHASES):
        for k in range(1, n):
            cell_copy(h, after(k), me).start()
        if h == 0:
            for k in range(1, n):
                fact_copy(after(k), me).start()

    low = lax.broadcasted_iota(jnp.int32, (2 * total, LANES), 1) < half
    for h in range(PHASES):
        own[h].wait()
        for k in range(1, n):
            cell_copy(h, before(k), before(k)).wait_recv()
        for s in range(n):
            x = got_cells[h, s].astype(jnp.float32)
            lines = []
            for a in range(PATCH_AZ):
                re = x[a * dates_here : (a + 1) * dates_here]
                start = (PATCH_AZ + a) * dates_here
                lines.append(jnp.concatenate([re, x[start : start + dates_here]], axis=0))
            for j, window in enumerate(block_transpose(lines, PATCH_RG)):
                z_ref[j, pl.ds(s * dates_here, dates_here), :] = window[:dates_here]
                z_ref[j, pl.ds(total + s * dates_here, dates_here), :] = window[dates_here:]

        def whiten(i, carry):
            for q in range(TOGETHER):
                z_ref[i * TOGETHER + q] = whiten_window(z_ref[i * TOGETHER + q].astype(jnp.bfloat16))
            return carry

        lax.fori_loop(0, windows // TOGETHER, whiten, 0)
        chunk = 16

        def back(r, carry):
            at = pl.ds(pl.multiple_of(r * chunk, chunk), chunk)
            first = lax.broadcasted_iota(jnp.int32, (chunk, LANES), 1) < half
            lines = block_transpose([z_ref[j, at, :] for j in range(windows)], PATCH_RG)
            for a in range(PATCH_AZ):
                turned = pltpu.roll(lines[a], half, 1)
                tiles_ref[a * 2, at, :] = jnp.where(first, lines[a], turned).astype(jnp.bfloat16)
                tiles_ref[a * 2 + 1, at, :] = jnp.where(first, turned, lines[a]).astype(jnp.bfloat16)
            return carry

        lax.fori_loop(0, 2 * total // chunk, back, 0)

        def message(o):
            return jnp.where(low, tiles_ref[table_ref[o * CAP]], tiles_ref[table_ref[o * CAP + 1]])

        def pack(k, carry):
            o = after(k)
            out_msg[h, o] = message(o)
            return carry

        lax.fori_loop(1, n, pack, 0)
        got_msg[h, me] = message(me)
        for k in range(1, n):
            msg_copy(h, after(k), me).start()

    total_ref[...] = jnp.zeros(total_ref.shape, jnp.float32)
    den_ref[...] = jnp.zeros(den_ref.shape, jnp.float32)
    apart = lax.broadcasted_iota(jnp.int32, (TILE, TILE), 0) - lax.broadcasted_iota(jnp.int32, (TILE, TILE), 1) + TILE
    lane = lax.broadcasted_iota(jnp.int32, (1, LANES), 1)
    map_row = lax.broadcasted_iota(jnp.int32, den_ref.shape, 0)
    blank = jnp.zeros((half, TILE), jnp.bfloat16)

    def gather(s):
        facts = got_facts[s].astype(jnp.float32)
        mine = got_facts[s, pl.ds(0, 1), :] == me
        place = lane.astype(jnp.float32)
        first = jnp.min(jnp.where(mine, place, 2.0 * LANES), axis=1, keepdims=True)
        last = jnp.max(jnp.where(mine, place, -1.0), axis=1, keepdims=True)
        columns, weights = [], []
        for i, at in enumerate((first, last)):
            picked = jnp.sum(jnp.where(place == at, facts, 0.0), axis=1, keepdims=True)
            slot, shift, corr = picked[1:2], picked[2:3].astype(jnp.int32), picked[3:4]
            if i:
                corr = jnp.where(last > first, corr, 0.0)
            step = (apart - shift) & (TILE - 1)
            circ = jnp.zeros((TILE, TILE), jnp.float32)
            for k in range(KW):
                circ = jnp.where(step == k, kern_ref[k], circ)
            circ = circ.astype(jnp.bfloat16)
            pieces = [circ[:half], blank, circ[half:], blank] if i == 0 else [blank, circ[:half], blank, circ[half:]]
            columns.append(jnp.concatenate(pieces, axis=0))
            weights.append(jnp.where(map_row == slot.astype(jnp.int32), corr, 0.0))
        x = jnp.concatenate([got_msg[h, s] for h in range(PHASES)], axis=1)
        moved = jnp.dot(x, jnp.concatenate(columns, axis=1), preferred_element_type=jnp.float32)
        den_ref[...] += weights[0] + weights[1]
        for m in range(MAP_DEV):
            total_ref[m] += (
                weights[0][m : m + 1] * moved[:, :TILE] + weights[1][m : m + 1] * moved[:, TILE:]
            )

    own[PHASES].wait()
    gather(me)

    def arrive(k, carry):
        s = before(k)
        fact_copy(s, s).wait_recv()
        for h in range(PHASES):
            msg_copy(h, s, s).wait_recv()
        gather(s)
        return carry

    lax.fori_loop(1, n, arrive, 0)
    for k in range(1, n):
        fact_copy(after(k), me).wait_send()
        for h in range(PHASES):
            cell_copy(h, after(k), me).wait_send()
            msg_copy(h, after(k), me).wait_send()


def shards(n, radar_stack, filter_taps, filter_lengths, resample_kernel, tile_owner, map_slot, correlation, offsets):
    dates_here, rows, ranges = radar_stack.shape[1:]
    dates = n * dates_here
    tile_count = tile_owner.shape[0]
    block = (PHASES, n, 2 * PATCH_AZ * dates_here, LANES)
    message = (PHASES, n, 2 * dates, LANES)
    facts = [x.reshape(1, tile_count) for x in (tile_owner, map_slot, offsets, correlation)]

    cells, known, table = pl.pallas_call(
        partial(filter_kernel, n),
        out_shape=[
            jax.ShapeDtypeStruct(block, jnp.bfloat16),
            jax.ShapeDtypeStruct((8, LANES), jnp.int32),
            jax.ShapeDtypeStruct((n * CAP,), jnp.int32),
        ],
        in_specs=[SMEM, SMEM] + [VMEM] * 6,
        out_specs=[VMEM, VMEM, SMEM],
        scratch_shapes=[pltpu.VMEM(block, jnp.float32), pltpu.SMEM((n,), jnp.int32)],
        compiler_params=pltpu.CompilerParams(vmem_limit_bytes=BIG),
        name="filter",
    )(filter_lengths, tile_owner.reshape(tile_count), radar_stack, filter_taps, *facts)
    dma = pltpu.SemaphoreType.DMA
    total, den = pl.pallas_call(
        partial(flow_kernel, n),
        out_shape=[
            jax.ShapeDtypeStruct((MAP_DEV, 2 * dates, TILE), jnp.float32),
            jax.ShapeDtypeStruct((MAP_DEV, TILE), jnp.float32),
        ],
        in_specs=[SMEM, SMEM, VMEM, VMEM],
        out_specs=[VMEM, VMEM],
        scratch_shapes=[
            pltpu.VMEM(block, jnp.bfloat16),
            pltpu.VMEM((n, 8, LANES), jnp.int32),
            pltpu.VMEM((LANES // PATCH_RG, 2 * dates, LANES), jnp.float32),
            pltpu.VMEM((tile_count, 2 * dates, LANES), jnp.bfloat16),
            pltpu.VMEM(message, jnp.bfloat16),
            pltpu.VMEM(message, jnp.bfloat16),
            dma((PHASES + 1,)),
            dma((n,)),
            dma((n,)),
            dma((PHASES, n)),
            dma((PHASES, n)),
            dma((PHASES, n)),
            dma((PHASES, n)),
        ],
        compiler_params=pltpu.CompilerParams(collective_id=0, has_side_effects=True, vmem_limit_bytes=BIG),
        name="flow",
    )(table, resample_kernel, cells, known)
    return total / jnp.maximum(den[:, :1, None], 1.0)


def solution(mesh):
    in_specs = (
        P(None, "date", "grp", None),
        P(None, "date", None),
        P("date"),
        P(),
        P(("grp", "date"), None),
        P(("grp", "date")),
        P(("grp", "date")),
        P(("grp", "date")),
    )
    out_specs = P(("grp", "date"), None, None)
    return jax.shard_map(
        partial(shards, mesh.shape["date"]), mesh=mesh, in_specs=in_specs, out_specs=out_specs, check_vma=False
    )
```

```python
from functools import partial

import jax
import jax.numpy as jnp
from jax import lax
from jax.experimental import pallas as pl
from jax.experimental.pallas import tpu as pltpu
from jax.sharding import PartitionSpec as P

PATCH_AZ = 8
PATCH_RG = 16
TILE = 128
KW = 4
CAP = 2
MAP_DEV = 8
LANES = 128
PHASES = 2
TOGETHER = 4
SWEEPS = 3

diag_load = 0.5
small_eps = 1e-05
MESH = pl.DeviceIdType.MESH
VMEM = pl.BlockSpec(memory_space=pltpu.VMEM)
SMEM = pl.BlockSpec(memory_space=pltpu.SMEM)
BIG = 60 * 1024 * 1024


def filter_kernel(n, len_ref, owner_ref, radar_ref, taps_ref, *refs):
    fact_refs, (out_ref, facts_ref, table_ref, rows_ref, seen_ref) = refs[:4], refs[4:]
    dates, rows = radar_ref.shape[1], radar_ref.shape[2]
    taps = taps_ref.shape[2]
    tile_count = owner_ref.shape[0]
    half = LANES // PHASES

    facts_ref[...] = jnp.full(facts_ref.shape, -1, jnp.int32)
    for i, fact in enumerate(fact_refs):
        facts_ref[pl.ds(i, 1), pl.ds(0, tile_count)] = fact[...]
    for o in range(n):
        seen_ref[o] = 0
        for i in range(CAP):
            table_ref[o * CAP + i] = 0
    for t in range(tile_count):
        owner = owner_ref[t]
        rank = seen_ref[owner]
        table_ref[owner * CAP + rank] = t
        seen_ref[owner] = rank + 1

    position = lax.broadcasted_iota(jnp.int32, (1, taps), 1)
    a_iota = lax.broadcasted_iota(jnp.int32, (rows, rows), 0)
    b_iota = lax.broadcasted_iota(jnp.int32, (rows, rows), 1)
    at = b_iota - a_iota + taps // 2
    inside = jnp.logical_and(at >= 0, at < taps)
    low = lax.broadcasted_iota(jnp.int32, (2 * rows, LANES), 1) < half
    for d in range(dates):

        def toeplitz(which):
            h = jnp.where(position < len_ref[d], taps_ref[which, pl.ds(d, 1), :], 0.0)
            wide = jnp.broadcast_to(h, (rows, taps))
            rolled = pltpu.roll(wide, taps // 2, 1, stride=1, stride_axis=0)
            full = jnp.concatenate([rolled] * (rows // taps), axis=1)
            return jnp.where(inside, full, 0.0)

        t_re, t_im = toeplitz(0), toeplitz(1)
        operator = jnp.concatenate(
            [jnp.concatenate([t_re, -t_im], axis=1), jnp.concatenate([t_im, t_re], axis=1)], axis=0
        ).astype(jnp.bfloat16)
        columns = jnp.concatenate([radar_ref[0, d], radar_ref[1, d]], axis=0)
        product = jnp.dot(operator, columns, preferred_element_type=jnp.float32)
        left, right = product[:, :LANES], product[:, LANES:]
        phases = (
            jnp.where(low, left, pltpu.roll(right, half, 1)),
            jnp.where(low, pltpu.roll(left, half, 1), right),
        )
        for h, phase in enumerate(phases):
            for p in range(n):
                for part in range(2):
                    top = part * rows + p * PATCH_AZ
                    rows_ref[h, p, pl.ds(part * PATCH_AZ * dates + d, PATCH_AZ, stride=dates), :] = phase[
                        top : top + PATCH_AZ
                    ]
    for h in range(PHASES):
        for p in range(n):
            out_ref[h, p] = rows_ref[h, p].astype(jnp.bfloat16)


def whiten_window(zt):
    looks, dates = zt.shape[0], zt.shape[1] // 2
    gram = lax.dot_general(zt, zt, (((0,), (0,)), ((), ())), preferred_element_type=jnp.float32)
    gram_re = (gram[:dates, :dates] + gram[dates:, dates:]) * (1.0 / looks)
    gram_im = (gram[dates:, :dates] - gram[:dates, dates:]) * (1.0 / looks)
    eye = lax.broadcasted_iota(jnp.int32, (dates, dates), 0) == lax.broadcasted_iota(
        jnp.int32, (dates, dates), 1
    )
    diagonal = jnp.where(eye, gram_re, 0.0)
    scale_col = lax.rsqrt(jnp.sum(diagonal, axis=1, keepdims=True) + small_eps)
    scale_row = lax.rsqrt(jnp.sum(diagonal, axis=0, keepdims=True) + small_eps)
    outer = scale_col * scale_row
    coher_re = gram_re * outer + jnp.where(eye, diag_load, 0.0)
    coher_im = gram_im * outer
    sums = jnp.sum(jnp.abs(coher_re) + jnp.abs(coher_im), axis=1, keepdims=True)
    over = 1.0 / jnp.max(sums, axis=0, keepdims=True)

    part_re, part_im = coher_re * over, coher_im * over
    w, rounded = zt.astype(jnp.float32), zt
    for stage in range(SWEEPS):
        re, im = part_re.astype(jnp.bfloat16), part_im.astype(jnp.bfloat16)
        top = jnp.concatenate([re, -im], axis=1)
        whole = jnp.concatenate([top, jnp.concatenate([im, re], axis=1)], axis=0)
        if stage < SWEEPS - 1:
            both = jnp.dot(jnp.concatenate([top, rounded], axis=0), whole, preferred_element_type=jnp.float32)
            part_re = 2.0 * part_re - both[:dates, :dates]
            part_im = 2.0 * part_im + both[:dates, dates:]
            applied = both[dates:]
        else:
            applied = jnp.dot(rounded, whole, preferred_element_type=jnp.float32)
        w = 2.0 * w - applied
        rounded = w.astype(jnp.bfloat16)
    return (w * over).astype(jnp.bfloat16)


def flow_kernel(n, table_ref, kern_ref, cells_ref, facts_ref, *refs):
    result_ref, got_cells, got_facts, cell_ref, z_ref, tiles_ref, out_msg, got_msg, total_ref, den_ref = refs[:10]
    own_sem, fact_send, fact_recv, cell_send, cell_recv, msg_send, msg_recv = refs[10:]
    me = lax.axis_index("date")
    rows = cells_ref.shape[2]
    dates_here = rows // (2 * PATCH_AZ)
    total = n * dates_here
    half = LANES // PHASES
    windows = LANES // PATCH_RG

    barrier = pltpu.get_barrier_semaphore()
    for k in range(1, n):
        pl.semaphore_signal(barrier, inc=1, device_id={"date": lax.rem(me + k, n)}, device_id_type=MESH)
    own = [pltpu.make_async_copy(cells_ref.at[h, me], got_cells.at[h, me], own_sem.at[h]) for h in range(PHASES)]
    own.append(pltpu.make_async_copy(facts_ref, got_facts.at[me], own_sem.at[PHASES]))
    for copy in own:
        copy.start()
    pl.semaphore_wait(barrier, n - 1)

    def remote(src, dst, send, recv, peer):
        return pltpu.make_async_remote_copy(
            src_ref=src, dst_ref=dst, send_sem=send, recv_sem=recv, device_id={"date": peer}, device_id_type=MESH
        )

    def fact_copy(peer, origin):
        return remote(facts_ref, got_facts.at[origin], fact_send.at[peer], fact_recv.at[origin], peer)

    def cell_copy(h, peer, origin):
        return remote(
            cells_ref.at[h, peer], got_cells.at[h, origin], cell_send.at[h, peer], cell_recv.at[h, origin], peer
        )

    def msg_copy(h, peer, origin):
        return remote(
            out_msg.at[h, peer], got_msg.at[h, origin], msg_send.at[h, peer], msg_recv.at[h, origin], peer
        )

    def partner(k):
        peer, bit = me, 1
        while bit < n:
            peer = peer + (k // bit) % 2 * (1 - (me // bit) % 2 * 2) * bit
            bit *= 2
        return peer

    far_first = range(n - 1, 0, -1)

    for h in range(PHASES):
        for k in far_first:
            cell_copy(h, partner(k), me).start()
        if h == 0:
            for k in far_first:
                fact_copy(partner(k), me).start()

    per_half = windows // 2
    for h in range(PHASES):
        own[h].wait()
        for k in far_first:
            cell_copy(h, partner(k), partner(k)).wait_recv()
        for s in range(n):
            cell_ref[s] = got_cells[h, s].astype(jnp.float32)
        for part in range(2):
            for a in range(PATCH_AZ):
                at = pl.ds((part * PATCH_AZ + a) * dates_here, dates_here)
                line = jnp.concatenate([cell_ref[s, at, :] for s in range(n)], axis=0).T.astype(jnp.bfloat16)
                for j in range(windows):
                    z_ref[j, a * PATCH_RG : (a + 1) * PATCH_RG, part * total : (part + 1) * total] = line[
                        j * PATCH_RG : (j + 1) * PATCH_RG
                    ]

        def whiten(i, carry):
            for q in range(TOGETHER):
                side = i * TOGETHER // per_half
                j = i * TOGETHER % per_half + q
                white = whiten_window(z_ref[i * TOGETHER + q])
                for a in range(PATCH_AZ):
                    tiles_ref[a * 2 + side, pl.ds(j * PATCH_RG, PATCH_RG), :] = white[
                        a * PATCH_RG : (a + 1) * PATCH_RG
                    ]
            return carry

        lax.fori_loop(0, windows // TOGETHER, whiten, 0)

        def message(o, i):
            return tiles_ref[table_ref[o * CAP + i]]

        def pack(k, carry):
            o = partner(k)
            for i in range(CAP):
                out_msg[h, o, pl.ds(i * half, half), :] = message(o, i)
            return carry

        lax.fori_loop(1, n, pack, 0)
        for i in range(CAP):
            got_msg[h, me, pl.ds(i * half, half), :] = message(me, i)
        for k in far_first:
            msg_copy(h, partner(k), me).start()

    total_ref[...] = jnp.zeros(total_ref.shape, jnp.float32)
    den_ref[...] = jnp.zeros(den_ref.shape, jnp.float32)
    apart = lax.broadcasted_iota(jnp.int32, (TILE, TILE), 1) - lax.broadcasted_iota(jnp.int32, (TILE, TILE), 0) + TILE
    lane = lax.broadcasted_iota(jnp.int32, (1, LANES), 1)
    map_row = lax.broadcasted_iota(jnp.int32, den_ref.shape, 0)

    def gather(s):
        facts = got_facts[s].astype(jnp.float32)
        mine = got_facts[s, pl.ds(0, 1), :] == me
        place = lane.astype(jnp.float32)
        first = jnp.min(jnp.where(mine, place, 2.0 * LANES), axis=1, keepdims=True)
        last = jnp.max(jnp.where(mine, place, -1.0), axis=1, keepdims=True)
        moved, weights = [], []
        for i, at in enumerate((first, last)):
            picked = jnp.sum(jnp.where(place == at, facts, 0.0), axis=1, keepdims=True)
            slot, shift, corr = picked[1:2], picked[2:3].astype(jnp.int32), picked[3:4]
            if i:
                corr = jnp.where(last > first, corr, 0.0)
            step = (apart - shift) & (TILE - 1)
            circ = jnp.zeros((TILE, TILE), jnp.float32)
            for k in range(KW):
                circ = jnp.where(step == k, kern_ref[k], circ)
            x = jnp.concatenate([got_msg[h, s, pl.ds(i * half, half), :] for h in range(PHASES)], axis=0)
            moved.append(jnp.dot(circ.astype(jnp.bfloat16), x, preferred_element_type=jnp.float32))
            weights.append(jnp.where(map_row == slot.astype(jnp.int32), corr, 0.0))
        den_ref[...] += weights[0] + weights[1]
        for m in range(MAP_DEV):
            total_ref[m] += weights[0][m : m + 1, :1] * moved[0] + weights[1][m : m + 1, :1] * moved[1]

    own[PHASES].wait()
    gather(me)

    def arrive(i, carry):
        s = partner(n - i)
        fact_copy(s, s).wait_recv()
        for h in range(PHASES):
            msg_copy(h, s, s).wait_recv()
        gather(s)
        return carry

    lax.fori_loop(1, n, arrive, 0)
    for m in range(MAP_DEV):
        result_ref[m] = (total_ref[m] / jnp.maximum(den_ref[m : m + 1, :1], 1.0)).T
    for k in far_first:
        fact_copy(partner(k), me).wait_send()
        for h in range(PHASES):
            cell_copy(h, partner(k), me).wait_send()
            msg_copy(h, partner(k), me).wait_send()


def shards(n, radar_stack, filter_taps, filter_lengths, resample_kernel, tile_owner, map_slot, correlation, offsets):
    dates_here, rows, ranges = radar_stack.shape[1:]
    dates = n * dates_here
    tile_count = tile_owner.shape[0]
    block = (PHASES, n, 2 * PATCH_AZ * dates_here, LANES)
    message = (PHASES, n, LANES, 2 * dates)
    facts = [x.reshape(1, tile_count) for x in (tile_owner, map_slot, offsets, correlation)]

    cells, known, table = pl.pallas_call(
        partial(filter_kernel, n),
        out_shape=[
            jax.ShapeDtypeStruct(block, jnp.bfloat16),
            jax.ShapeDtypeStruct((8, LANES), jnp.int32),
            jax.ShapeDtypeStruct((n * CAP,), jnp.int32),
        ],
        in_specs=[SMEM, SMEM] + [VMEM] * 6,
        out_specs=[VMEM, VMEM, SMEM],
        scratch_shapes=[pltpu.VMEM(block, jnp.float32), pltpu.SMEM((n,), jnp.int32)],
        compiler_params=pltpu.CompilerParams(vmem_limit_bytes=BIG),
        name="filter",
    )(filter_lengths, tile_owner.reshape(tile_count), radar_stack, filter_taps, *facts)
    dma = pltpu.SemaphoreType.DMA
    return pl.pallas_call(
        partial(flow_kernel, n),
        out_shape=jax.ShapeDtypeStruct((MAP_DEV, 2 * dates, TILE), jnp.float32),
        in_specs=[SMEM, SMEM, VMEM, VMEM],
        out_specs=VMEM,
        scratch_shapes=[
            pltpu.VMEM(block, jnp.bfloat16),
            pltpu.VMEM((n, 8, LANES), jnp.int32),
            pltpu.VMEM(block[1:], jnp.float32),
            pltpu.VMEM((LANES // PATCH_RG, LANES, 2 * dates), jnp.bfloat16),
            pltpu.VMEM((tile_count, LANES // PHASES, 2 * dates), jnp.bfloat16),
            pltpu.VMEM(message, jnp.bfloat16),
            pltpu.VMEM(message, jnp.bfloat16),
            pltpu.VMEM((MAP_DEV, TILE, 2 * dates), jnp.float32),
            pltpu.VMEM((MAP_DEV, TILE), jnp.float32),
            dma((PHASES + 1,)),
            dma((n,)),
            dma((n,)),
            dma((PHASES, n)),
            dma((PHASES, n)),
            dma((PHASES, n)),
            dma((PHASES, n)),
        ],
        compiler_params=pltpu.CompilerParams(collective_id=0, has_side_effects=True, vmem_limit_bytes=BIG),
        name="flow",
    )(table, resample_kernel, cells, known)


def solution(mesh):
    in_specs = (
        P(None, "date", "grp", None),
        P(None, "date", None),
        P("date"),
        P(),
        P(("grp", "date"), None),
        P(("grp", "date")),
        P(("grp", "date")),
        P(("grp", "date")),
    )
    out_specs = P(("grp", "date"), None, None)
    return jax.shard_map(
        partial(shards, mesh.shape["date"]), mesh=mesh, in_specs=in_specs, out_specs=out_specs, check_vma=False
    )
```

```python
from functools import partial

import jax
import jax.numpy as jnp
from jax import lax
from jax.experimental import pallas as pl
from jax.experimental.pallas import tpu as pltpu
from jax.sharding import PartitionSpec as P

PATCH_AZ = 8
PATCH_RG = 16
TILE = 128
KW = 4
CAP = 2
MAP_DEV = 8
LANES = 128
PHASES = 2
TOGETHER = 4
SWEEPS = 3

diag_load = 0.5
small_eps = 1e-05
MESH = pl.DeviceIdType.MESH
VMEM = pl.BlockSpec(memory_space=pltpu.VMEM)
SMEM = pl.BlockSpec(memory_space=pltpu.SMEM)
BIG = 32 * 1024 * 1024


def whiten_window(zt):
    looks, dates = zt.shape[0], zt.shape[1] // 2
    gram = lax.dot_general(zt, zt, (((0,), (0,)), ((), ())), preferred_element_type=jnp.float32)
    gram_re = (gram[:dates, :dates] + gram[dates:, dates:]) * (1.0 / looks)
    gram_im = (gram[dates:, :dates] - gram[:dates, dates:]) * (1.0 / looks)
    eye = lax.broadcasted_iota(jnp.int32, (dates, dates), 0) == lax.broadcasted_iota(
        jnp.int32, (dates, dates), 1
    )
    diagonal = jnp.where(eye, gram_re, 0.0)
    scale_col = lax.rsqrt(jnp.sum(diagonal, axis=1, keepdims=True) + small_eps)
    scale_row = lax.rsqrt(jnp.sum(diagonal, axis=0, keepdims=True) + small_eps)
    outer = scale_col * scale_row
    coher_re = gram_re * outer + jnp.where(eye, diag_load, 0.0)
    coher_im = gram_im * outer
    sums = jnp.sum(jnp.abs(coher_re) + jnp.abs(coher_im), axis=1, keepdims=True)
    over = 1.0 / jnp.max(sums, axis=0, keepdims=True)

    part_re, part_im = coher_re * over, coher_im * over
    w, rounded = zt.astype(jnp.float32), zt
    for stage in range(SWEEPS):
        re, im = part_re.astype(jnp.bfloat16), part_im.astype(jnp.bfloat16)
        top = jnp.concatenate([re, -im], axis=1)
        whole = jnp.concatenate([top, jnp.concatenate([im, re], axis=1)], axis=0)
        if stage < SWEEPS - 1:
            both = jnp.dot(jnp.concatenate([top, rounded], axis=0), whole, preferred_element_type=jnp.float32)
            part_re = 2.0 * part_re - both[:dates, :dates]
            part_im = 2.0 * part_im + both[:dates, dates:]
            applied = both[dates:]
        else:
            applied = jnp.dot(rounded, whole, preferred_element_type=jnp.float32)
        w = 2.0 * w - applied
        rounded = w.astype(jnp.bfloat16)
    return (w * over).astype(jnp.bfloat16)


def flow_kernel(n, len_ref, owner_ref, kern_ref, radar_ref, taps_ref, *refs):
    fact_refs, refs = refs[:4], refs[4:]
    result_ref, cells_ref, got_cells, facts_ref, got_facts, cell_ref, z_ref, tiles_ref, out_msg, got_msg = refs[:10]
    total_ref, den_ref, operator_ref, table_ref = refs[10:14]
    own_sem, fact_send, fact_recv, cell_send, cell_recv, msg_send, msg_recv = refs[14:]
    me = lax.axis_index("date")
    dates_here, rows = radar_ref.shape[1], radar_ref.shape[2]
    taps, tile_count = taps_ref.shape[2], owner_ref.shape[0]
    total = n * dates_here
    half = LANES // PHASES
    windows = LANES // PATCH_RG

    barrier = pltpu.get_barrier_semaphore()
    for k in range(1, n):
        pl.semaphore_signal(barrier, inc=1, device_id={"date": lax.rem(me + k, n)}, device_id_type=MESH)
    own = [pltpu.make_async_copy(cells_ref.at[h, me], got_cells.at[h, me], own_sem.at[h]) for h in range(PHASES)]
    own.append(pltpu.make_async_copy(facts_ref, got_facts.at[me], own_sem.at[PHASES]))

    def remote(src, dst, send, recv, peer):
        return pltpu.make_async_remote_copy(
            src_ref=src, dst_ref=dst, send_sem=send, recv_sem=recv, device_id={"date": peer}, device_id_type=MESH
        )

    def fact_copy(peer, origin):
        return remote(facts_ref, got_facts.at[origin], fact_send.at[peer], fact_recv.at[origin], peer)

    def cell_copy(h, peer, origin):
        return remote(
            cells_ref.at[h, peer], got_cells.at[h, origin], cell_send.at[h, peer], cell_recv.at[h, origin], peer
        )

    def msg_copy(h, peer, origin):
        return remote(
            out_msg.at[h, peer], got_msg.at[h, origin], msg_send.at[h, peer], msg_recv.at[h, origin], peer
        )

    def partner(k):
        peer, bit = me, 1
        while bit < n:
            peer = peer + (k // bit) % 2 * (1 - (me // bit) % 2 * 2) * bit
            bit *= 2
        return peer

    far_first = range(n - 1, 0, -1)

    facts_ref[...] = jnp.full(facts_ref.shape, -1, jnp.int32)
    for i, fact in enumerate(fact_refs):
        facts_ref[pl.ds(i, 1), pl.ds(0, tile_count)] = fact[...]
    position = lax.broadcasted_iota(jnp.int32, (1, taps), 1)
    a_iota = lax.broadcasted_iota(jnp.int32, (rows, rows), 0)
    b_iota = lax.broadcasted_iota(jnp.int32, (rows, rows), 1)
    tap_at = b_iota - a_iota + taps // 2
    inside = jnp.logical_and(tap_at >= 0, tap_at < taps)
    low = lax.broadcasted_iota(jnp.int32, (2 * rows, LANES), 1) < half

    def toeplitz(d, which):
        kept = jnp.where(position < len_ref[d], taps_ref[which, pl.ds(d, 1), :], 0.0)
        rolled = pltpu.roll(jnp.broadcast_to(kept, (rows, taps)), taps // 2, 1, stride=1, stride_axis=0)
        return jnp.where(inside, jnp.concatenate([rolled] * (rows // taps), axis=1), 0.0)

    for h in range(PHASES):
        for d in range(dates_here):
            if h == 0:
                t_re, t_im = toeplitz(d, 0), toeplitz(d, 1)
                operator_ref[d] = jnp.concatenate(
                    [jnp.concatenate([t_re, -t_im], axis=1), jnp.concatenate([t_im, t_re], axis=1)], axis=0
                ).astype(jnp.bfloat16)
            columns = jnp.concatenate([radar_ref[0, d], radar_ref[1, d]], axis=0).astype(jnp.float32)
            sides = [columns[:, c * LANES : (c + 1) * LANES] for c in range(2)]
            sides[1 - h] = pltpu.roll(sides[1 - h], half, 1)
            product = jnp.dot(
                operator_ref[d],
                jnp.where(low, sides[0], sides[1]).astype(jnp.bfloat16),
                preferred_element_type=jnp.float32,
            )
            for p in range(n):
                for part in range(2):
                    top = part * rows + p * PATCH_AZ
                    cell_ref[p, pl.ds(part * PATCH_AZ * dates_here + d, PATCH_AZ, stride=dates_here), :] = product[
                        top : top + PATCH_AZ
                    ]
        for p in range(n):
            cells_ref[h, p] = cell_ref[p].astype(jnp.bfloat16)
        if h == 0:
            pl.semaphore_wait(barrier, n - 1)
        for k in far_first:
            cell_copy(h, partner(k), me).start()
        own[h].start()
        if h == 0:
            for k in far_first:
                fact_copy(partner(k), me).start()
            own[PHASES].start()

    owners = [owner_ref[t] for t in range(tile_count)]
    for o in range(n):
        first, last = 0, 0
        for t in range(tile_count):
            last = jnp.where(owners[t] == o, t, last)
            first = jnp.where(owners[tile_count - 1 - t] == o, tile_count - 1 - t, first)
        table_ref[o * CAP] = first
        table_ref[o * CAP + 1] = last

    per_half = windows // 2
    for h in range(PHASES):
        own[h].wait()
        for k in far_first:
            cell_copy(h, partner(k), partner(k)).wait_recv()
        for s in range(n):
            cell_ref[s] = got_cells[h, s].astype(jnp.float32)
        for part in range(2):
            for a in range(PATCH_AZ):
                at = pl.ds((part * PATCH_AZ + a) * dates_here, dates_here)
                line = jnp.concatenate([cell_ref[s, at, :] for s in range(n)], axis=0).T.astype(jnp.bfloat16)
                for j in range(windows):
                    z_ref[j, a * PATCH_RG : (a + 1) * PATCH_RG, part * total : (part + 1) * total] = line[
                        j * PATCH_RG : (j + 1) * PATCH_RG
                    ]

        def whiten(i, carry):
            for q in range(TOGETHER):
                side = i * TOGETHER // per_half
                j = i * TOGETHER % per_half + q
                white = whiten_window(z_ref[i * TOGETHER + q])
                for a in range(PATCH_AZ):
                    tiles_ref[a * 2 + side, pl.ds(j * PATCH_RG, PATCH_RG), :] = white[
                        a * PATCH_RG : (a + 1) * PATCH_RG
                    ]
            return carry

        lax.fori_loop(0, windows // TOGETHER, whiten, 0)

        def message(o, i):
            return tiles_ref[table_ref[o * CAP + i]]

        def pack(k, carry):
            o = partner(k)
            for i in range(CAP):
                out_msg[h, o, pl.ds(i * half, half), :] = message(o, i)
            return carry

        lax.fori_loop(1, n, pack, 0)
        for i in range(CAP):
            got_msg[h, me, pl.ds(i * half, half), :] = message(me, i)
        for k in far_first:
            msg_copy(h, partner(k), me).start()

    total_ref[...] = jnp.zeros(total_ref.shape, jnp.float32)
    den_ref[...] = jnp.zeros(den_ref.shape, jnp.float32)
    apart = lax.broadcasted_iota(jnp.int32, (TILE, TILE), 1) - lax.broadcasted_iota(jnp.int32, (TILE, TILE), 0) + TILE
    lane = lax.broadcasted_iota(jnp.int32, (1, LANES), 1)
    map_row = lax.broadcasted_iota(jnp.int32, den_ref.shape, 0)

    def gather(s):
        facts = got_facts[s].astype(jnp.float32)
        mine = got_facts[s, pl.ds(0, 1), :] == me
        place = lane.astype(jnp.float32)
        first = jnp.min(jnp.where(mine, place, 2.0 * LANES), axis=1, keepdims=True)
        last = jnp.max(jnp.where(mine, place, -1.0), axis=1, keepdims=True)
        moved, weights = [], []
        for i, at in enumerate((first, last)):
            picked = jnp.sum(jnp.where(place == at, facts, 0.0), axis=1, keepdims=True)
            slot, shift, corr = picked[1:2], picked[2:3].astype(jnp.int32), picked[3:4]
            if i:
                corr = jnp.where(last > first, corr, 0.0)
            step = (apart - shift) & (TILE - 1)
            circ = jnp.zeros((TILE, TILE), jnp.float32)
            for k in range(KW):
                circ = jnp.where(step == k, kern_ref[k], circ)
            x = jnp.concatenate([got_msg[h, s, pl.ds(i * half, half), :] for h in range(PHASES)], axis=0)
            moved.append(jnp.dot(circ.astype(jnp.bfloat16), x, preferred_element_type=jnp.float32))
            weights.append(jnp.where(map_row == slot.astype(jnp.int32), corr, 0.0))
        den_ref[...] += weights[0] + weights[1]
        for m in range(MAP_DEV):
            total_ref[m] += weights[0][m : m + 1, :1] * moved[0] + weights[1][m : m + 1, :1] * moved[1]

    own[PHASES].wait()
    gather(me)

    def arrive(i, carry):
        s = partner(i)
        fact_copy(s, s).wait_recv()
        for h in range(PHASES):
            msg_copy(h, s, s).wait_recv()
        gather(s)
        return carry

    near = min(4, n)
    lax.fori_loop(1, near, arrive, 0)
    lax.fori_loop(near, n, lambda i, carry: arrive(n - 1 + near - i, carry), 0)
    for m in range(MAP_DEV):
        result_ref[m] = (total_ref[m] / jnp.maximum(den_ref[m : m + 1, :1], 1.0)).T
    for k in far_first:
        fact_copy(partner(k), me).wait_send()
        for h in range(PHASES):
            cell_copy(h, partner(k), me).wait_send()
            msg_copy(h, partner(k), me).wait_send()


def shards(n, radar_stack, filter_taps, filter_lengths, resample_kernel, tile_owner, map_slot, correlation, offsets):
    dates_here, rows, ranges = radar_stack.shape[1:]
    dates = n * dates_here
    tile_count = tile_owner.shape[0]
    block = (PHASES, n, 2 * PATCH_AZ * dates_here, LANES)
    message = (PHASES, n, LANES, 2 * dates)
    facts = [x.reshape(1, tile_count) for x in (tile_owner, map_slot, offsets, correlation)]

    dma = pltpu.SemaphoreType.DMA
    return pl.pallas_call(
        partial(flow_kernel, n),
        out_shape=jax.ShapeDtypeStruct((MAP_DEV, 2 * dates, TILE), jnp.float32),
        in_specs=[SMEM, SMEM, SMEM] + [VMEM] * 6,
        out_specs=VMEM,
        scratch_shapes=[
            pltpu.VMEM(block, jnp.bfloat16),
            pltpu.VMEM(block, jnp.bfloat16),
            pltpu.VMEM((8, LANES), jnp.int32),
            pltpu.VMEM((n, 8, LANES), jnp.int32),
            pltpu.VMEM(block[1:], jnp.float32),
            pltpu.VMEM((LANES // PATCH_RG, LANES, 2 * dates), jnp.bfloat16),
            pltpu.VMEM((tile_count, LANES // PHASES, 2 * dates), jnp.bfloat16),
            pltpu.VMEM(message, jnp.bfloat16),
            pltpu.VMEM(message, jnp.bfloat16),
            pltpu.VMEM((MAP_DEV, TILE, 2 * dates), jnp.float32),
            pltpu.VMEM((MAP_DEV, TILE), jnp.float32),
            pltpu.VMEM((dates_here, 2 * rows, 2 * rows), jnp.bfloat16),
            pltpu.SMEM((n * CAP,), jnp.int32),
            dma((PHASES + 1,)),
            dma((n,)),
            dma((n,)),
            dma((PHASES, n)),
            dma((PHASES, n)),
            dma((PHASES, n)),
            dma((PHASES, n)),
        ],
        compiler_params=pltpu.CompilerParams(collective_id=0, has_side_effects=True, vmem_limit_bytes=BIG),
        name="flow",
    )(filter_lengths, tile_owner.reshape(tile_count), resample_kernel, radar_stack, filter_taps, *facts)


def solution(mesh):
    in_specs = (
        P(None, "date", "grp", None),
        P(None, "date", None),
        P("date"),
        P(),
        P(("grp", "date"), None),
        P(("grp", "date")),
        P(("grp", "date")),
        P(("grp", "date")),
    )
    out_specs = P(("grp", "date"), None, None)
    return jax.shard_map(
        partial(shards, mesh.shape["date"]), mesh=mesh, in_specs=in_specs, out_specs=out_specs, check_vma=False
    )
```

```python
from functools import partial

import jax
import jax.numpy as jnp
from jax import lax
from jax.experimental import pallas as pl
from jax.experimental.pallas import tpu as pltpu
from jax.sharding import PartitionSpec as P

PATCH_AZ = 8
PATCH_RG = 16
TILE = 128
KW = 4
CAP = 2
MAP_DEV = 8
LANES = 128
PHASES = 2
TOGETHER = 4
SWEEPS = 3

diag_load = 0.5
small_eps = 1e-05
MESH = pl.DeviceIdType.MESH
VMEM = pl.BlockSpec(memory_space=pltpu.VMEM)
HBM = pl.BlockSpec(memory_space=pltpu.MemorySpace.HBM)
BIG = 32 * 1024 * 1024


def whiten_window(zt):
    looks, dates = zt.shape[0], zt.shape[1] // 2
    gram = lax.dot_general(zt, zt, (((0,), (0,)), ((), ())), preferred_element_type=jnp.float32)
    gram_re = (gram[:dates, :dates] + gram[dates:, dates:]) * (1.0 / looks)
    gram_im = (gram[dates:, :dates] - gram[:dates, dates:]) * (1.0 / looks)
    eye = lax.broadcasted_iota(jnp.int32, (dates, dates), 0) == lax.broadcasted_iota(
        jnp.int32, (dates, dates), 1
    )
    diagonal = jnp.where(eye, gram_re, 0.0)
    scale_col = lax.rsqrt(jnp.sum(diagonal, axis=1, keepdims=True) + small_eps)
    scale_row = lax.rsqrt(jnp.sum(diagonal, axis=0, keepdims=True) + small_eps)
    outer = scale_col * scale_row
    coher_re = gram_re * outer + jnp.where(eye, diag_load, 0.0)
    coher_im = gram_im * outer
    sums = jnp.sum(jnp.abs(coher_re) + jnp.abs(coher_im), axis=1, keepdims=True)
    over = 1.0 / jnp.max(sums, axis=0, keepdims=True)

    part_re, part_im = coher_re * over, coher_im * over
    w, rounded = zt.astype(jnp.float32), zt
    for stage in range(SWEEPS):
        re, im = part_re.astype(jnp.bfloat16), part_im.astype(jnp.bfloat16)
        top = jnp.concatenate([re, -im], axis=1)
        whole = jnp.concatenate([top, jnp.concatenate([im, re], axis=1)], axis=0)
        if stage < SWEEPS - 1:
            both = jnp.dot(jnp.concatenate([top, rounded], axis=0), whole, preferred_element_type=jnp.float32)
            part_re = 2.0 * part_re - both[:dates, :dates]
            part_im = 2.0 * part_im + both[:dates, dates:]
            applied = both[dates:]
        else:
            applied = jnp.dot(rounded, whole, preferred_element_type=jnp.float32)
        w = 2.0 * w - applied
        rounded = w.astype(jnp.bfloat16)
    return (w * over).astype(jnp.bfloat16)


def flow_kernel(n, *refs):
    inputs, refs = refs[:9], refs[9:]
    result_ref, cells_ref, got_cells, facts_ref, got_facts, cell_ref, z_ref, tiles_ref, out_msg, got_msg = refs[:10]
    total_ref, den_ref, operator_ref, table_ref = refs[10:14]
    local, refs = refs[14:23], refs[23:]
    len_ref, owner_ref, kern_ref, radar_ref, taps_ref = local[:5]
    fact_refs = local[5:]
    own_sem, fact_send, fact_recv, cell_send, cell_recv, msg_send, msg_recv, load_sem = refs
    me = lax.axis_index("date")
    dates_here, rows = radar_ref.shape[1], radar_ref.shape[2]
    taps, tile_count = taps_ref.shape[2], owner_ref.shape[0]
    total = n * dates_here
    half = LANES // PHASES
    windows = LANES // PATCH_RG

    barrier = pltpu.get_barrier_semaphore()
    loads = [pltpu.make_async_copy(x, y, load_sem.at[i]) for i, (x, y) in enumerate(zip(inputs, local))]
    for load in loads:
        load.start()
    for k in range(1, n):
        pl.semaphore_signal(barrier, inc=1, device_id={"date": lax.rem(me + k, n)}, device_id_type=MESH)
    own = [pltpu.make_async_copy(cells_ref.at[h, me], got_cells.at[h, me], own_sem.at[h]) for h in range(PHASES)]
    own.append(pltpu.make_async_copy(facts_ref, got_facts.at[me], own_sem.at[PHASES]))

    def remote(src, dst, send, recv, peer):
        return pltpu.make_async_remote_copy(
            src_ref=src, dst_ref=dst, send_sem=send, recv_sem=recv, device_id={"date": peer}, device_id_type=MESH
        )

    def fact_copy(peer, origin):
        return remote(facts_ref, got_facts.at[origin], fact_send.at[peer], fact_recv.at[origin], peer)

    def cell_copy(h, peer, origin):
        return remote(
            cells_ref.at[h, peer], got_cells.at[h, origin], cell_send.at[h, peer], cell_recv.at[h, origin], peer
        )

    def msg_copy(h, peer, origin):
        return remote(
            out_msg.at[h, peer], got_msg.at[h, origin], msg_send.at[h, peer], msg_recv.at[h, origin], peer
        )

    def partner(k):
        peer, bit = me, 1
        while bit < n:
            peer = peer + (k // bit) % 2 * (1 - (me // bit) % 2 * 2) * bit
            bit *= 2
        return peer

    def turn(i):
        return n - 1 - i // 2 - i % 2 * (n // 2)

    peers = [turn(i) for i in range(n - 1)]

    for load in loads:
        load.wait()
    facts_ref[...] = jnp.full(facts_ref.shape, -1, jnp.int32)
    for i, fact in enumerate(fact_refs):
        facts_ref[pl.ds(i, 1), pl.ds(0, tile_count)] = fact[...]
    position = lax.broadcasted_iota(jnp.int32, (1, taps), 1)
    a_iota = lax.broadcasted_iota(jnp.int32, (rows, rows), 0)
    b_iota = lax.broadcasted_iota(jnp.int32, (rows, rows), 1)
    tap_at = b_iota - a_iota + taps // 2
    inside = jnp.logical_and(tap_at >= 0, tap_at < taps)
    low = lax.broadcasted_iota(jnp.int32, (2 * rows, LANES), 1) < half

    def toeplitz(d, which):
        kept = jnp.where(position < len_ref[d], taps_ref[which, pl.ds(d, 1), :], 0.0)
        rolled = pltpu.roll(jnp.broadcast_to(kept, (rows, taps)), taps // 2, 1, stride=1, stride_axis=0)
        return jnp.where(inside, jnp.concatenate([rolled] * (rows // taps), axis=1), 0.0)

    for h in range(PHASES):
        for d in range(dates_here):
            if h == 0:
                t_re, t_im = toeplitz(d, 0), toeplitz(d, 1)
                operator_ref[d] = jnp.concatenate(
                    [jnp.concatenate([t_re, -t_im], axis=1), jnp.concatenate([t_im, t_re], axis=1)], axis=0
                ).astype(jnp.bfloat16)
            columns = jnp.concatenate([radar_ref[0, d], radar_ref[1, d]], axis=0).astype(jnp.float32)
            sides = [columns[:, c * LANES : (c + 1) * LANES] for c in range(2)]
            sides[1 - h] = pltpu.roll(sides[1 - h], half, 1)
            product = jnp.dot(
                operator_ref[d],
                jnp.where(low, sides[0], sides[1]).astype(jnp.bfloat16),
                preferred_element_type=jnp.float32,
            )
            for p in range(n):
                for part in range(2):
                    top = part * rows + p * PATCH_AZ
                    cell_ref[p, pl.ds(part * PATCH_AZ * dates_here + d, PATCH_AZ, stride=dates_here), :] = product[
                        top : top + PATCH_AZ
                    ]
        for p in range(n):
            cells_ref[h, p] = cell_ref[p].astype(jnp.bfloat16)
        if h == 0:
            pl.semaphore_wait(barrier, n - 1)
        for k in peers:
            cell_copy(h, partner(k), me).start()
        own[h].start()
        if h == 0:
            for k in peers:
                fact_copy(partner(k), me).start()
            own[PHASES].start()

    owners = [owner_ref[t] for t in range(tile_count)]
    for o in range(n):
        first, last = 0, 0
        for t in range(tile_count):
            last = jnp.where(owners[t] == o, t, last)
            first = jnp.where(owners[tile_count - 1 - t] == o, tile_count - 1 - t, first)
        table_ref[o * CAP] = first
        table_ref[o * CAP + 1] = last

    per_half = windows // 2
    for h in range(PHASES):
        own[h].wait()
        for k in peers:
            cell_copy(h, partner(k), partner(k)).wait_recv()
        for s in range(n):
            cell_ref[s] = got_cells[h, s].astype(jnp.float32)
        for part in range(2):
            for a in range(PATCH_AZ):
                at = pl.ds((part * PATCH_AZ + a) * dates_here, dates_here)
                line = jnp.concatenate([cell_ref[s, at, :] for s in range(n)], axis=0).T.astype(jnp.bfloat16)
                for j in range(windows):
                    z_ref[j, a * PATCH_RG : (a + 1) * PATCH_RG, part * total : (part + 1) * total] = line[
                        j * PATCH_RG : (j + 1) * PATCH_RG
                    ]

        def whiten(i, carry):
            for q in range(TOGETHER):
                side = i * TOGETHER // per_half
                j = i * TOGETHER % per_half + q
                white = whiten_window(z_ref[i * TOGETHER + q])
                for a in range(PATCH_AZ):
                    tiles_ref[a * 2 + side, pl.ds(j * PATCH_RG, PATCH_RG), :] = white[
                        a * PATCH_RG : (a + 1) * PATCH_RG
                    ]
            return carry

        lax.fori_loop(0, windows // TOGETHER, whiten, 0)

        def message(o, i):
            return tiles_ref[table_ref[o * CAP + i]]

        def pack(k, carry):
            o = partner(k)
            for i in range(CAP):
                out_msg[h, o, pl.ds(i * half, half), :] = message(o, i)
            return carry

        lax.fori_loop(1, n, pack, 0)
        for i in range(CAP):
            got_msg[h, me, pl.ds(i * half, half), :] = message(me, i)
        for k in peers:
            msg_copy(h, partner(k), me).start()

    total_ref[...] = jnp.zeros(total_ref.shape, jnp.float32)
    den_ref[...] = jnp.zeros(den_ref.shape, jnp.float32)
    apart = lax.broadcasted_iota(jnp.int32, (TILE, TILE), 1) - lax.broadcasted_iota(jnp.int32, (TILE, TILE), 0) + TILE
    lane = lax.broadcasted_iota(jnp.int32, (1, LANES), 1)
    map_row = lax.broadcasted_iota(jnp.int32, den_ref.shape, 0)

    def gather(s):
        facts = got_facts[s].astype(jnp.float32)
        mine = got_facts[s, pl.ds(0, 1), :] == me
        place = lane.astype(jnp.float32)
        first = jnp.min(jnp.where(mine, place, 2.0 * LANES), axis=1, keepdims=True)
        last = jnp.max(jnp.where(mine, place, -1.0), axis=1, keepdims=True)
        moved, weights = [], []
        for i, at in enumerate((first, last)):
            picked = jnp.sum(jnp.where(place == at, facts, 0.0), axis=1, keepdims=True)
            slot, shift, corr = picked[1:2], picked[2:3].astype(jnp.int32), picked[3:4]
            if i:
                corr = jnp.where(last > first, corr, 0.0)
            step = (apart - shift) & (TILE - 1)
            circ = jnp.zeros((TILE, TILE), jnp.float32)
            for k in range(KW):
                circ = jnp.where(step == k, kern_ref[k], circ)
            x = jnp.concatenate([got_msg[h, s, pl.ds(i * half, half), :] for h in range(PHASES)], axis=0)
            moved.append(jnp.dot(circ.astype(jnp.bfloat16), x, preferred_element_type=jnp.float32))
            weights.append(jnp.where(map_row == slot.astype(jnp.int32), corr, 0.0))
        den_ref[...] += weights[0] + weights[1]
        for m in range(MAP_DEV):
            total_ref[m] += weights[0][m : m + 1, :1] * moved[0] + weights[1][m : m + 1, :1] * moved[1]

    own[PHASES].wait()
    gather(me)

    def arrive(i, carry):
        s = partner(turn(i))
        fact_copy(s, s).wait_recv()
        for h in range(PHASES):
            msg_copy(h, s, s).wait_recv()
        gather(s)
        return carry

    lax.fori_loop(0, n - 1, arrive, 0)
    for m in range(MAP_DEV):
        result_ref[m] = (total_ref[m] / jnp.maximum(den_ref[m : m + 1, :1], 1.0)).T
    for k in peers:
        fact_copy(partner(k), me).wait_send()
        for h in range(PHASES):
            cell_copy(h, partner(k), me).wait_send()
            msg_copy(h, partner(k), me).wait_send()


def shards(n, radar_stack, filter_taps, filter_lengths, resample_kernel, tile_owner, map_slot, correlation, offsets):
    dates_here, rows, ranges = radar_stack.shape[1:]
    dates = n * dates_here
    tile_count = tile_owner.shape[0]
    block = (PHASES, n, 2 * PATCH_AZ * dates_here, LANES)
    message = (PHASES, n, LANES, 2 * dates)
    facts = [x.reshape(1, tile_count) for x in (tile_owner, map_slot, offsets, correlation)]

    dma = pltpu.SemaphoreType.DMA
    return pl.pallas_call(
        partial(flow_kernel, n),
        out_shape=jax.ShapeDtypeStruct((MAP_DEV, 2 * dates, TILE), jnp.float32),
        in_specs=[HBM] * 9,
        out_specs=VMEM,
        scratch_shapes=[
            pltpu.VMEM(block, jnp.bfloat16),
            pltpu.VMEM(block, jnp.bfloat16),
            pltpu.VMEM((8, LANES), jnp.int32),
            pltpu.VMEM((n, 8, LANES), jnp.int32),
            pltpu.VMEM(block[1:], jnp.float32),
            pltpu.VMEM((LANES // PATCH_RG, LANES, 2 * dates), jnp.bfloat16),
            pltpu.VMEM((tile_count, LANES // PHASES, 2 * dates), jnp.bfloat16),
            pltpu.VMEM(message, jnp.bfloat16),
            pltpu.VMEM(message, jnp.bfloat16),
            pltpu.VMEM((MAP_DEV, TILE, 2 * dates), jnp.float32),
            pltpu.VMEM((MAP_DEV, TILE), jnp.float32),
            pltpu.VMEM((dates_here, 2 * rows, 2 * rows), jnp.bfloat16),
            pltpu.SMEM((n * CAP,), jnp.int32),
            pltpu.SMEM(filter_lengths.shape, jnp.int32),
            pltpu.SMEM((tile_count,), jnp.int32),
            pltpu.SMEM(resample_kernel.shape, jnp.float32),
            pltpu.VMEM(radar_stack.shape, radar_stack.dtype),
            pltpu.VMEM(filter_taps.shape, jnp.float32),
            pltpu.VMEM((1, tile_count), jnp.int32),
            pltpu.VMEM((1, tile_count), jnp.int32),
            pltpu.VMEM((1, tile_count), jnp.int32),
            pltpu.VMEM((1, tile_count), jnp.int32),
            dma((PHASES + 1,)),
            dma((n,)),
            dma((n,)),
            dma((PHASES, n)),
            dma((PHASES, n)),
            dma((PHASES, n)),
            dma((PHASES, n)),
            dma((9,)),
        ],
        compiler_params=pltpu.CompilerParams(collective_id=0, has_side_effects=True, vmem_limit_bytes=BIG),
        name="flow",
    )(*[pltpu.with_memory_space_constraint(x, pltpu.MemorySpace.HBM) for x in (filter_lengths, tile_owner.reshape(tile_count), resample_kernel, radar_stack, filter_taps, *facts)])


def solution(mesh):
    in_specs = (
        P(None, "date", "grp", None),
        P(None, "date", None),
        P("date"),
        P(),
        P(("grp", "date"), None),
        P(("grp", "date")),
        P(("grp", "date")),
        P(("grp", "date")),
    )
    out_specs = P(("grp", "date"), None, None)
    return jax.shard_map(
        partial(shards, mesh.shape["date"]), mesh=mesh, in_specs=in_specs, out_specs=out_specs, check_vma=False
    )
```

```python
from functools import partial

import jax
import jax.numpy as jnp
from jax import lax
from jax.experimental import pallas as pl
from jax.experimental.pallas import tpu as pltpu
from jax.sharding import PartitionSpec as P

PATCH_AZ = 8
PATCH_RG = 16
TILE = 128
KW = 4
CAP = 2
MAP_DEV = 8
LANES = 128
PHASES = 2
TOGETHER = 4
SWEEPS = 3

diag_load = 0.5
small_eps = 1e-05
MESH = pl.DeviceIdType.MESH
VMEM = pl.BlockSpec(memory_space=pltpu.VMEM)
HBM = pl.BlockSpec(memory_space=pltpu.MemorySpace.HBM)
BIG = 32 * 1024 * 1024


def whiten_window(zt):
    looks, dates = zt.shape[0], zt.shape[1] // 2
    gram = lax.dot_general(zt, zt, (((0,), (0,)), ((), ())), preferred_element_type=jnp.float32)
    gram_re = (gram[:dates, :dates] + gram[dates:, dates:]) * (1.0 / looks)
    gram_im = (gram[dates:, :dates] - gram[:dates, dates:]) * (1.0 / looks)
    eye = lax.broadcasted_iota(jnp.int32, (dates, dates), 0) == lax.broadcasted_iota(
        jnp.int32, (dates, dates), 1
    )
    diagonal = jnp.where(eye, gram_re, 0.0)
    scale_col = lax.rsqrt(jnp.sum(diagonal, axis=1, keepdims=True) + small_eps)
    scale_row = lax.rsqrt(jnp.sum(diagonal, axis=0, keepdims=True) + small_eps)
    outer = scale_col * scale_row
    coher_re = gram_re * outer + jnp.where(eye, diag_load, 0.0)
    coher_im = gram_im * outer
    sums = jnp.sum(jnp.abs(coher_re) + jnp.abs(coher_im), axis=1, keepdims=True)
    over = 1.0 / jnp.max(sums, axis=0, keepdims=True)

    part_re, part_im = coher_re * over, coher_im * over
    w, rounded = zt.astype(jnp.float32), zt
    for stage in range(SWEEPS):
        re, im = part_re.astype(jnp.bfloat16), part_im.astype(jnp.bfloat16)
        top = jnp.concatenate([re, -im], axis=1)
        whole = jnp.concatenate([top, jnp.concatenate([im, re], axis=1)], axis=0)
        if stage < SWEEPS - 1:
            both = jnp.dot(jnp.concatenate([top, rounded], axis=0), whole, preferred_element_type=jnp.float32)
            part_re = 2.0 * part_re - both[:dates, :dates]
            part_im = 2.0 * part_im + both[:dates, dates:]
            applied = both[dates:]
        else:
            applied = jnp.dot(rounded, whole, preferred_element_type=jnp.float32)
        w = 2.0 * w - applied
        rounded = w.astype(jnp.bfloat16)
    return (w * over).astype(jnp.bfloat16)


def flow_kernel(n, *refs):
    inputs, refs = refs[:9], refs[9:]
    result_ref, cells_ref, got_cells, facts_ref, got_facts, cell_ref, z_ref, tiles_ref, out_msg, got_msg = refs[:10]
    total_ref, den_ref, operator_ref, table_ref = refs[10:14]
    local, refs = refs[14:23], refs[23:]
    len_ref, owner_ref, kern_ref, radar_ref, taps_ref = local[:5]
    fact_refs = local[5:]
    own_sem, fact_send, fact_recv, cell_send, cell_recv, msg_send, msg_recv, load_sem = refs
    me = lax.axis_index("date")
    dates_here, rows = radar_ref.shape[1], radar_ref.shape[2]
    taps, tile_count = taps_ref.shape[2], owner_ref.shape[0]
    total = n * dates_here
    half = LANES // PHASES
    windows = LANES // PATCH_RG

    barrier = pltpu.get_barrier_semaphore()
    loads = [pltpu.make_async_copy(x, y, load_sem.at[i]) for i, (x, y) in enumerate(zip(inputs, local))]
    for load in loads:
        load.start()
    for k in range(1, n):
        pl.semaphore_signal(barrier, inc=1, device_id={"date": lax.rem(me + k, n)}, device_id_type=MESH)
    own = [pltpu.make_async_copy(cells_ref.at[h, me], got_cells.at[h, me], own_sem.at[h]) for h in range(PHASES)]
    own.append(pltpu.make_async_copy(facts_ref, got_facts.at[me], own_sem.at[PHASES]))

    def remote(src, dst, send, recv, peer):
        return pltpu.make_async_remote_copy(
            src_ref=src, dst_ref=dst, send_sem=send, recv_sem=recv, device_id={"date": peer}, device_id_type=MESH
        )

    def fact_copy(peer, origin):
        return remote(facts_ref, got_facts.at[origin], fact_send.at[peer], fact_recv.at[origin], peer)

    def cell_copy(h, peer, origin):
        return remote(
            cells_ref.at[h, peer], got_cells.at[h, origin], cell_send.at[h, peer], cell_recv.at[h, origin], peer
        )

    def msg_copy(h, peer, origin):
        return remote(
            out_msg.at[h, peer], got_msg.at[h, origin], msg_send.at[h, peer], msg_recv.at[h, origin], peer
        )

    def partner(k):
        peer, bit = me, 1
        while bit < n:
            peer = peer + (k // bit) % 2 * (1 - (me // bit) % 2 * 2) * bit
            bit *= 2
        return peer

    def turn(i):
        return n - 1 - i // 2 - i % 2 * (n // 2)

    peers = [turn(i) for i in range(n - 1)]

    radar_load = loads.pop(3)
    for load in loads:
        load.wait()
    facts_ref[...] = jnp.full(facts_ref.shape, -1, jnp.int32)
    for i, fact in enumerate(fact_refs):
        facts_ref[pl.ds(i, 1), pl.ds(0, tile_count)] = fact[...]
    position = lax.broadcasted_iota(jnp.int32, (1, taps), 1)
    a_iota = lax.broadcasted_iota(jnp.int32, (rows, rows), 0)
    b_iota = lax.broadcasted_iota(jnp.int32, (rows, rows), 1)
    tap_at = b_iota - a_iota + taps // 2
    inside = jnp.logical_and(tap_at >= 0, tap_at < taps)
    low = lax.broadcasted_iota(jnp.int32, (2 * rows, LANES), 1) < half

    def toeplitz(d, which):
        kept = jnp.where(position < len_ref[d], taps_ref[which, pl.ds(d, 1), :], 0.0)
        rolled = pltpu.roll(jnp.broadcast_to(kept, (rows, taps)), taps // 2, 1, stride=1, stride_axis=0)
        return jnp.where(inside, jnp.concatenate([rolled] * (rows // taps), axis=1), 0.0)

    for h in range(PHASES):
        for d in range(dates_here):
            if h == 0:
                t_re, t_im = toeplitz(d, 0), toeplitz(d, 1)
                operator_ref[d] = jnp.concatenate(
                    [jnp.concatenate([t_re, -t_im], axis=1), jnp.concatenate([t_im, t_re], axis=1)], axis=0
                ).astype(jnp.bfloat16)
            if h == 0 and d == 0:
                radar_load.wait()
            columns = jnp.concatenate([radar_ref[0, d], radar_ref[1, d]], axis=0).astype(jnp.float32)
            sides = [columns[:, c * LANES : (c + 1) * LANES] for c in range(2)]
            sides[1 - h] = pltpu.roll(sides[1 - h], half, 1)
            product = jnp.dot(
                operator_ref[d],
                jnp.where(low, sides[0], sides[1]).astype(jnp.bfloat16),
                preferred_element_type=jnp.float32,
            )
            for p in range(n):
                for part in range(2):
                    top = part * rows + p * PATCH_AZ
                    cell_ref[p, pl.ds(part * PATCH_AZ * dates_here + d, PATCH_AZ, stride=dates_here), :] = product[
                        top : top + PATCH_AZ
                    ]
        for p in range(n):
            cells_ref[h, p] = cell_ref[p].astype(jnp.bfloat16)
        if h == 0:
            pl.semaphore_wait(barrier, n - 1)
        for k in peers:
            cell_copy(h, partner(k), me).start()
        own[h].start()
        if h == 0:
            for k in peers:
                fact_copy(partner(k), me).start()
            own[PHASES].start()

    owners = [owner_ref[t] for t in range(tile_count)]
    for o in range(n):
        first, last = 0, 0
        for t in range(tile_count):
            last = jnp.where(owners[t] == o, t, last)
            first = jnp.where(owners[tile_count - 1 - t] == o, tile_count - 1 - t, first)
        table_ref[o * CAP] = first
        table_ref[o * CAP + 1] = last

    per_half = windows // 2
    for h in range(PHASES):
        own[h].wait()
        for k in peers:
            cell_copy(h, partner(k), partner(k)).wait_recv()
        for s in range(n):
            cell_ref[s] = got_cells[h, s].astype(jnp.float32)
        for part in range(2):
            for a in range(PATCH_AZ):
                at = pl.ds((part * PATCH_AZ + a) * dates_here, dates_here)
                line = jnp.concatenate([cell_ref[s, at, :] for s in range(n)], axis=0).T.astype(jnp.bfloat16)
                for j in range(windows):
                    z_ref[j, a * PATCH_RG : (a + 1) * PATCH_RG, part * total : (part + 1) * total] = line[
                        j * PATCH_RG : (j + 1) * PATCH_RG
                    ]

        def whiten(i, carry):
            for q in range(TOGETHER):
                side = i * TOGETHER // per_half
                j = i * TOGETHER % per_half + q
                white = whiten_window(z_ref[i * TOGETHER + q])
                for a in range(PATCH_AZ):
                    tiles_ref[a * 2 + side, pl.ds(j * PATCH_RG, PATCH_RG), :] = white[
                        a * PATCH_RG : (a + 1) * PATCH_RG
                    ]
            return carry

        lax.fori_loop(0, windows // TOGETHER, whiten, 0)

        def message(o, i):
            return tiles_ref[table_ref[o * CAP + i]]

        def pack(k, carry):
            o = partner(k)
            for i in range(CAP):
                out_msg[h, o, pl.ds(i * half, half), :] = message(o, i)
            return carry

        lax.fori_loop(1, n, pack, 0)
        for i in range(CAP):
            got_msg[h, me, pl.ds(i * half, half), :] = message(me, i)
        for k in peers:
            msg_copy(h, partner(k), me).start()

    total_ref[...] = jnp.zeros(total_ref.shape, jnp.float32)
    den_ref[...] = jnp.zeros(den_ref.shape, jnp.float32)
    apart = lax.broadcasted_iota(jnp.int32, (TILE, TILE), 1) - lax.broadcasted_iota(jnp.int32, (TILE, TILE), 0) + TILE
    lane = lax.broadcasted_iota(jnp.int32, (1, LANES), 1)
    map_row = lax.broadcasted_iota(jnp.int32, den_ref.shape, 0)

    def gather(s):
        facts = got_facts[s].astype(jnp.float32)
        mine = got_facts[s, pl.ds(0, 1), :] == me
        place = lane.astype(jnp.float32)
        first = jnp.min(jnp.where(mine, place, 2.0 * LANES), axis=1, keepdims=True)
        last = jnp.max(jnp.where(mine, place, -1.0), axis=1, keepdims=True)
        moved, weights = [], []
        for i, at in enumerate((first, last)):
            picked = jnp.sum(jnp.where(place == at, facts, 0.0), axis=1, keepdims=True)
            slot, shift, corr = picked[1:2], picked[2:3].astype(jnp.int32), picked[3:4]
            if i:
                corr = jnp.where(last > first, corr, 0.0)
            step = (apart - shift) & (TILE - 1)
            circ = jnp.zeros((TILE, TILE), jnp.float32)
            for k in range(KW):
                circ = jnp.where(step == k, kern_ref[k], circ)
            x = jnp.concatenate([got_msg[h, s, pl.ds(i * half, half), :] for h in range(PHASES)], axis=0)
            moved.append(jnp.dot(circ.astype(jnp.bfloat16), x, preferred_element_type=jnp.float32))
            weights.append(jnp.where(map_row == slot.astype(jnp.int32), corr, 0.0))
        den_ref[...] += weights[0] + weights[1]
        for m in range(MAP_DEV):
            total_ref[m] += weights[0][m : m + 1, :1] * moved[0] + weights[1][m : m + 1, :1] * moved[1]

    own[PHASES].wait()
    gather(me)

    def arrive(i, carry):
        s = partner(turn(i))
        fact_copy(s, s).wait_recv()
        for h in range(PHASES):
            msg_copy(h, s, s).wait_recv()
        gather(s)
        return carry

    lax.fori_loop(0, n - 1, arrive, 0)
    for m in range(MAP_DEV):
        result_ref[m] = (total_ref[m] / jnp.maximum(den_ref[m : m + 1, :1], 1.0)).T
    for k in peers:
        fact_copy(partner(k), me).wait_send()
        for h in range(PHASES):
            cell_copy(h, partner(k), me).wait_send()
            msg_copy(h, partner(k), me).wait_send()


def shards(n, radar_stack, filter_taps, filter_lengths, resample_kernel, tile_owner, map_slot, correlation, offsets):
    dates_here, rows, ranges = radar_stack.shape[1:]
    dates = n * dates_here
    tile_count = tile_owner.shape[0]
    block = (PHASES, n, 2 * PATCH_AZ * dates_here, LANES)
    message = (PHASES, n, LANES, 2 * dates)
    facts = [x.reshape(1, tile_count) for x in (tile_owner, map_slot, offsets, correlation)]

    dma = pltpu.SemaphoreType.DMA
    return pl.pallas_call(
        partial(flow_kernel, n),
        out_shape=jax.ShapeDtypeStruct((MAP_DEV, 2 * dates, TILE), jnp.float32),
        in_specs=[HBM] * 9,
        out_specs=VMEM,
        scratch_shapes=[
            pltpu.VMEM(block, jnp.bfloat16),
            pltpu.VMEM(block, jnp.bfloat16),
            pltpu.VMEM((8, LANES), jnp.int32),
            pltpu.VMEM((n, 8, LANES), jnp.int32),
            pltpu.VMEM(block[1:], jnp.float32),
            pltpu.VMEM((LANES // PATCH_RG, LANES, 2 * dates), jnp.bfloat16),
            pltpu.VMEM((tile_count, LANES // PHASES, 2 * dates), jnp.bfloat16),
            pltpu.VMEM(message, jnp.bfloat16),
            pltpu.VMEM(message, jnp.bfloat16),
            pltpu.VMEM((MAP_DEV, TILE, 2 * dates), jnp.float32),
            pltpu.VMEM((MAP_DEV, TILE), jnp.float32),
            pltpu.VMEM((dates_here, 2 * rows, 2 * rows), jnp.bfloat16),
            pltpu.SMEM((n * CAP,), jnp.int32),
            pltpu.SMEM(filter_lengths.shape, jnp.int32),
            pltpu.SMEM((tile_count,), jnp.int32),
            pltpu.SMEM(resample_kernel.shape, jnp.float32),
            pltpu.VMEM(radar_stack.shape, radar_stack.dtype),
            pltpu.VMEM(filter_taps.shape, jnp.float32),
            pltpu.VMEM((1, tile_count), jnp.int32),
            pltpu.VMEM((1, tile_count), jnp.int32),
            pltpu.VMEM((1, tile_count), jnp.int32),
            pltpu.VMEM((1, tile_count), jnp.int32),
            dma((PHASES + 1,)),
            dma((n,)),
            dma((n,)),
            dma((PHASES, n)),
            dma((PHASES, n)),
            dma((PHASES, n)),
            dma((PHASES, n)),
            dma((9,)),
        ],
        compiler_params=pltpu.CompilerParams(collective_id=0, has_side_effects=True, vmem_limit_bytes=BIG),
        name="flow",
    )(*[pltpu.with_memory_space_constraint(x, pltpu.MemorySpace.HBM) for x in (filter_lengths, tile_owner.reshape(tile_count), resample_kernel, radar_stack, filter_taps, *facts)])


def solution(mesh):
    in_specs = (
        P(None, "date", "grp", None),
        P(None, "date", None),
        P("date"),
        P(),
        P(("grp", "date"), None),
        P(("grp", "date")),
        P(("grp", "date")),
        P(("grp", "date")),
    )
    out_specs = P(("grp", "date"), None, None)
    return jax.shard_map(
        partial(shards, mesh.shape["date"]), mesh=mesh, in_specs=in_specs, out_specs=out_specs, check_vma=False
    )
```
